256 devices in a mesh: lat: 64 (over y, z, x_lo), depth: 4 (over x_hi, core).
Axes of the slice: x: 4 (x_hi: 2, x_lo: 2; x = x_hi * 2 + x_lo), y: 4, z: 8, core: 2. Of those that a mesh axis runs over, the one named last changes fastest.
Arguments:
- thermal_anomaly: float32 [128, 256, 2048], P('depth', 'lat'), may hold values from -6 to 6
- water_anomaly: float32 [128, 256, 2048], P('depth', 'lat'), may hold values from -6 to 6
- substrate_class_label: int32 [256, 2048], P('lat'), may hold values from 0 to 11
- sideways_thermal_spread: float32 [12], replicated, may hold values from 0.1 to 0.6
- sideways_water_factors: float32 [12], replicated, may hold values from 0.1 to 0.9
- thermal_solve_matrix: float32 [128, 128], replicated, may hold values from -0.3 to 1.3, as said below
- water_solve_matrix: float32 [128, 128], replicated, may hold values from -0.3 to 1.3, as said below
Outputs:
- temperature_next: float32 [128, 256, 2048], P('depth', 'lat')
- moisture_next: float32 [128, 256, 2048], P('depth', 'lat')
The draws below stay inside these ranges and needn't reach their ends.
Inputs may be any that keep to these rules, and one draw needn't show every extreme that they name: `thermal_solve_matrix`: a dense matrix with unit diagonal. `water_solve_matrix`: a dense matrix with unit diagonal.
All inputs are finite; a program needn't handle non-finite values.
Results may differ from the reference program's by a relative error of at most 0.00007.
Values sent between devices are 32-bit elements; how exact they have to be, the bound alone decides.
A program may use at most 128 MiB of HBM per device.

```python
import math
import jax
import jax.numpy as jnp
from jax import lax

VERTICAL_POINTS = 128
CLASSES = 12
LSUB = 4
PLOTS_PER_LINE = 2048
MESH_LINES_TOTAL = 256


def solve_matrix(key):
    reach = 1.2 / VERTICAL_POINTS ** 0.5
    noise = jax.random.uniform(key, (VERTICAL_POINTS, VERTICAL_POINTS), jnp.float32, -reach, reach)
    diagonal = jnp.arange(VERTICAL_POINTS)[:, None] == jnp.arange(VERTICAL_POINTS)[None, :]
    return jnp.where(diagonal, 1.0, noise).astype(jnp.float32)


def draw_thermal_solve_matrix(key, part):
    return solve_matrix(jax.random.fold_in(key, 11))


def draw_water_solve_matrix(key, part):
    return solve_matrix(jax.random.fold_in(key, 23))


def plant(values, key, smallest, high):
    extent = values.shape
    index_at = [jax.random.randint(jax.random.fold_in(key, axis), (), 0, extent[axis]) for axis in range(len(extent))]
    values = values.at[tuple(index_at)].set(smallest)
    longest = extent.index(max(extent))
    index_at[longest] = (index_at[longest] + 1) % extent[longest]
    return values.at[tuple(index_at)].set(high)


def shard_levels(own_key, shape, pieces, smallest, high):
    loudness = 1.0
    for position, parts in pieces:
        heights = jax.random.uniform(jax.random.fold_in(jax.random.fold_in(own_key, 6), position), (parts,), jnp.float32, smallest / len(pieces), high / len(pieces))
        loudness = loudness * jnp.repeat(jnp.exp(heights), shape[position] // parts).reshape((-1,) + (1,) * (len(shape) - 1 - position))
    return loudness


def normal_values(own_key, shape, scale, bound, split=(), dtype=jnp.bfloat16):
    values = jax.random.normal(own_key, shape, jnp.float32) * scale
    if len(split) > 0:
        values = shard_levels(own_key, shape, split, -0.22, 0.18) * values
    return jnp.clip(values, min=-bound, max=bound).astype(dtype)


def setup_inputs(seed: int = 0) -> dict:
    key_of = jax.random.split(jax.random.key(seed), 8)
    return {
        "thermal_anomaly": normal_values(key_of[0], (VERTICAL_POINTS, MESH_LINES_TOTAL, PLOTS_PER_LINE), 1.0, 6.0, ((0, 4), (1, 64)), jnp.float32),
        "water_anomaly": normal_values(key_of[1], (VERTICAL_POINTS, MESH_LINES_TOTAL, PLOTS_PER_LINE), 1.0, 6.0, ((0, 4), (1, 64)), jnp.float32),
        "substrate_class_label": plant(jax.random.randint(key_of[2], (MESH_LINES_TOTAL, PLOTS_PER_LINE), 0, CLASSES), jax.random.fold_in(key_of[2], 1), 0, CLASSES - 1).astype(jnp.int32),
        "sideways_thermal_spread": jnp.clip(jnp.exp(jax.random.uniform(key_of[3], (CLASSES,), jnp.float32, math.log(0.1), math.log(0.6))), 0.1, 0.6),
        "sideways_water_factors": jnp.clip(jnp.exp(jax.random.uniform(key_of[4], (CLASSES,), jnp.float32, math.log(0.1), math.log(0.9))), 0.1, 0.9),
        "thermal_solve_matrix": draw_thermal_solve_matrix(jax.random.fold_in(key_of[7], 71), 0),
        "water_solve_matrix": draw_water_solve_matrix(jax.random.fold_in(key_of[7], 71), 0),
    }


RATE = 0.25


def cheb_matrix(count):
    index = jnp.arange(count).astype(jnp.float32)
    nodes = jnp.cos(jnp.pi * index / (count - 1))
    ends = jnp.where((index == 0) | (index == count - 1), 2.0, 1.0)
    signs = jnp.where(jnp.arange(count) % 2 == 0, 1.0, -1.0)
    weight = (ends * signs).astype(jnp.float32)
    diagonal = jnp.arange(count)[:, None] == jnp.arange(count)[None, :]
    spread = nodes[:, None] - nodes[None, :]
    off = weight[:, None] / weight[None, :] / jnp.where(diagonal, 1.0, spread)
    off = jnp.where(diagonal, 0.0, off)
    return off - jnp.diag(jnp.sum(off, axis=1)), nodes


def lateral_sum(after, before, centre):
    zeros = jnp.zeros_like(centre[..., :1])
    east = jnp.concatenate([centre[..., 1:], zeros], axis=-1)
    west = jnp.concatenate([zeros, centre[..., :-1]], axis=-1)
    return after + before + east + west - 4.0 * centre


def advance(profile_snapshot, lap, kappa_heat, kappa_moist):
    wet = profile_snapshot[1]
    kappa_t = kappa_heat * (1.0 + 0.5 * wet * wet / (1.0 + wet * wet))
    return jnp.stack([profile_snapshot[0] + RATE * kappa_t * lap[0], profile_snapshot[1] + RATE * kappa_moist * lap[1]])


def column_step(fields, deriv, nodes, thermal_solve_matrix, water_solve_matrix):
    high = lax.Precision.HIGHEST
    scale = (1.0 - nodes * nodes) / deriv.shape[0]
    drain = jnp.einsum("zk,k...->z...", deriv, fields[2], precision=high)
    drain = drain * scale.reshape((-1,) + (1,) * (fields.ndim - 2))
    rhs_heat = fields[0] - 0.25 * drain
    rhs_wet = fields[1] + 0.5 * drain
    new_heat = jnp.einsum("zk,k...->z...", thermal_solve_matrix, rhs_heat, precision=high)
    new_wet = jnp.einsum("zk,k...->z...", water_solve_matrix, rhs_wet, precision=high)
    return jnp.stack([new_heat, new_wet])


def reference(thermal_anomaly, water_anomaly, substrate_class_label, sideways_thermal_spread, sideways_water_factors, thermal_solve_matrix, water_solve_matrix):
    kappa_heat = sideways_thermal_spread[substrate_class_label]
    kappa_moist = sideways_water_factors[substrate_class_label]

    def vertical_level(pair):
        profile_snapshot = jnp.stack([pair[0], pair[1]])
        for step in range(LSUB):
            zeros = jnp.zeros_like(profile_snapshot[:, :1])
            after = jnp.concatenate([profile_snapshot[:, 1:], zeros], axis=1)
            before = jnp.concatenate([zeros, profile_snapshot[:, :-1]], axis=1)
            lap = lateral_sum(after, before, profile_snapshot)
            profile_snapshot = advance(profile_snapshot, lap, kappa_heat, kappa_moist)
        return profile_snapshot

    profile_snapshots = lax.map(vertical_level, (thermal_anomaly, water_anomaly))
    deriv, nodes = cheb_matrix(VERTICAL_POINTS)

    def row(item):
        heat_row, wet_row, kappa_row = item
        fields = jnp.stack([heat_row, wet_row, kappa_row[None, :] * wet_row])
        return column_step(fields, deriv, nodes, thermal_solve_matrix, water_solve_matrix)

    heat_rows = jnp.transpose(profile_snapshots[:, 0], (1, 0, 2))
    wet_rows = jnp.transpose(profile_snapshots[:, 1], (1, 0, 2))
    result = lax.map(row, (heat_rows, wet_rows, kappa_moist))
    return jnp.transpose(result[:, 0], (1, 0, 2)), jnp.transpose(result[:, 1], (1, 0, 2))
```

```python
import functools

import jax
import jax.numpy as jnp
import numpy as np
from jax import lax
from jax.experimental import pallas as pl
from jax.experimental.pallas import tpu as pltpu
from jax.sharding import PartitionSpec as P

MESH = pl.DeviceIdType.MESH
LEVELS = 128
CLASSES = 12
LSUB = 4
CHUNKS = 2
LANES = 128
SLAB = 32
PIECE = 272
OFFSETS = [(h, l, c) for h in (0, 1) for l in (0, 1) for c in (0, 1)]


def scaled_derivative():
    f32 = np.float32
    index = np.arange(LEVELS).astype(f32)
    nodes = np.cos(f32(np.pi) * index / f32(LEVELS - 1)).astype(f32)
    ends = np.where((index == 0) | (index == LEVELS - 1), 2.0, 1.0)
    signs = np.where(np.arange(LEVELS) % 2 == 0, 1.0, -1.0)
    weight = (ends * signs).astype(f32)
    diagonal = np.eye(LEVELS, dtype=bool)
    spread = nodes[:, None] - nodes[None, :]
    off = weight[:, None] / weight[None, :] / np.where(diagonal, f32(1), spread)
    off = np.where(diagonal, f32(0), off)
    deriv = off - np.diag(np.sum(off, axis=1))
    scale = (f32(1) - nodes * nodes) / f32(LEVELS)
    return (scale[:, None] * deriv).astype(f32)


def flip(value, bit):
    return 1 - value if bit else value


def kernel(
    pairs,
    heat_ref, wet_ref, label_ref, spread_ref, factor_ref, thermal_ref, water_ref, deriv_ref,
    heat_out, wet_out,
    slab, block, piece, kloc, ksend, kgot, coef, kmid, state, solved, result, mats,
    load_sem, own_sem, xsend, xrecv, zsend, zrecv, kown_sem, kx_sem, kz_sem, kzrecv, rown_sem, rsend, rrecv, store_sem,
):
    my_lat = lax.axis_index("lat")
    my_d = lax.axis_index("depth")
    pair, lo = my_lat // 2, my_lat % 2
    hi, core = my_d // 2, my_d % 2
    me = lo * 4 + my_d
    has_before, has_after = pair > 0, pair < pairs - 1

    def place(o):
        h, l, c = o
        lo2 = flip(lo, l)
        d2 = flip(hi, h) * 2 + flip(core, c)
        return lo2, d2, (pair * 2 + lo2, d2)

    loads = []
    for f, src in enumerate((heat_ref, wet_ref)):
        for r in range(4):
            loads.append(pltpu.make_async_copy(src.at[:, r, :], slab.at[f, r], load_sem.at[f * 4 + r]))
    for cp in loads:
        cp.start()

    barrier = pltpu.get_barrier_semaphore()
    for o in OFFSETS[1:]:
        pl.semaphore_signal(barrier, inc=1, device_id=place(o)[2], device_id_type=MESH)

    @pl.when(has_before)
    def _():
        pl.semaphore_signal(barrier, inc=1, device_id=(my_lat - 2, my_d), device_id_type=MESH)

    @pl.when(has_after)
    def _():
        pl.semaphore_signal(barrier, inc=1, device_id=(my_lat + 2, my_d), device_id_type=MESH)

    lane = lax.broadcasted_iota(jnp.int32, (8, LANES), 1)
    right, left = lane < 4, lane >= LANES - 4

    kloc[0] = jnp.zeros((8, LANES), jnp.float32)
    kloc[17] = jnp.zeros((8, LANES), jnp.float32)
    for t in range(16):
        label = label_ref[:, t * LANES:(t + 1) * LANES]
        kh = jnp.zeros((4, LANES), jnp.float32)
        km = jnp.zeros((4, LANES), jnp.float32)
        for n in range(CLASSES):
            kh = jnp.where(label == n, spread_ref[n], kh)
            km = jnp.where(label == n, factor_ref[n], km)
        kloc[t + 1, 0:4] = kh
        kloc[t + 1, 4:8] = km

    def kblock(t):
        main = kloc[t + 1]
        edge = jnp.where(right, kloc[t + 2], jnp.where(left, kloc[t], 0.0))
        return main, edge

    partner = (0, 1, 0)
    plo, pd, pdev = place(partner)
    for k in range(CHUNKS):
        main, edge = kblock(k * 8 + plo * 4 + pd)
        ksend[k, 0] = main
        ksend[k, 1] = edge
        main, edge = kblock(k * 8 + me)
        kgot[1 + lo, k, 0] = main
        kgot[1 + lo, k, 1] = edge

    @pl.when(jnp.logical_not(has_before))
    def _():
        kgot[0] = jnp.zeros((CHUNKS, 2, 8, LANES), jnp.float32)

        @pl.loop(0, CHUNKS * 4)
        def _(i):
            piece[i // 4, 0, i % 4] = jnp.zeros((PIECE, LANES), jnp.float32)

    @pl.when(jnp.logical_not(has_after))
    def _():
        kgot[3] = jnp.zeros((CHUNKS, 2, 8, LANES), jnp.float32)

        @pl.loop(0, CHUNKS * 4)
        def _(i):
            piece[i // 4, 3, i % 4] = jnp.zeros((PIECE, LANES), jnp.float32)

    for cp in loads:
        cp.wait()

    def build(k):
        @pl.loop(0, 8)
        def _(j):
            t = k * 8 + j
            here = pl.multiple_of(t * LANES, LANES)
            before = pl.multiple_of(jnp.maximum(t - 1, 0) * LANES, LANES)
            after = pl.multiple_of(jnp.minimum(t + 1, 15) * LANES, LANES)
            keep_left = jnp.logical_and(left, t > 0)
            keep_right = jnp.logical_and(right, t < 15)
            for f in range(2):
                packed = jnp.zeros((8, LANES), jnp.float32)
                for r in range(4):
                    for q in range(4):
                        g = r * 4 + q
                        rows = pl.ds(q * 8, 8)
                        block[t, pl.ds((f * 16 + g) * 8, 8), :] = slab[f, r, rows, pl.ds(here, LANES)]
                        edge = jnp.where(
                            keep_right,
                            slab[f, r, rows, pl.ds(after, LANES)],
                            jnp.where(keep_left, slab[f, r, rows, pl.ds(before, LANES)], 0.0),
                        )
                        packed = packed + (pltpu.roll(edge, 8 * g, 1) if g else edge)
                block[t, pl.ds(256 + f * 8, 8), :] = packed

    def x_copy(k, o):
        lo2, d2, dev = place(o)
        n = OFFSETS.index(o)
        return pltpu.make_async_remote_copy(
            src_ref=block.at[k * 8 + lo2 * 4 + d2],
            dst_ref=piece.at[k, 1 + lo, o[0] * 2 + o[2]],
            send_sem=xsend.at[k, n],
            recv_sem=xrecv.at[k, n],
            device_id=dev,
            device_id_type=MESH,
        )

    def x_arrival(k, o):
        lo2, d2, dev = place(o)
        n = OFFSETS.index(o)
        return pltpu.make_async_remote_copy(
            src_ref=block.at[k * 8 + lo2 * 4 + d2],
            dst_ref=piece.at[k, 1 + lo2, o[0] * 2 + o[2]],
            send_sem=xsend.at[k, n],
            recv_sem=xrecv.at[k, n],
            device_id=dev,
            device_id_type=MESH,
        )

    def own_copy(k):
        return pltpu.make_async_copy(block.at[k * 8 + me], piece.at[k, 1 + lo, 0], own_sem.at[k])

    def forward_copy(k, o, s):
        n = OFFSETS.index(o)
        q = o[0] * 2 + o[2]
        return pltpu.make_async_remote_copy(
            src_ref=piece.at[k, 1 + s, q],
            dst_ref=piece.at[k, 3 if s == 0 else 0, q],
            send_sem=zsend.at[k, n],
            recv_sem=zrecv.at[k, q, s],
            device_id=(my_lat - 2 if s == 0 else my_lat + 2, my_d),
            device_id_type=MESH,
        )

    def forward(k, o, act):
        lo2 = flip(lo, o[1])

        @pl.when(jnp.logical_and(lo2 == 0, has_before))
        def _():
            act(forward_copy(k, o, 0))

        @pl.when(jnp.logical_and(lo2 == 1, has_after))
        def _():
            act(forward_copy(k, o, 1))

    def halo_wait(k, q):
        o = (q // 2, 0, q % 2)

        @pl.when(has_after)
        def _():
            forward_copy(k, o, 0).wait_recv()

        @pl.when(has_before)
        def _():
            forward_copy(k, o, 1).wait_recv()

    def k_forward(s, act):
        @pl.when(has_before if s == 0 else has_after)
        def _():
            act(
                pltpu.make_async_remote_copy(
                    src_ref=kgot.at[1 + s],
                    dst_ref=kgot.at[3 if s == 0 else 0],
                    send_sem=kz_sem.at[s],
                    recv_sem=kzrecv.at[s],
                    device_id=(my_lat - 2 if s == 0 else my_lat + 2, my_d),
                    device_id_type=MESH,
                )
            )

    def k_copy(strip):
        return pltpu.make_async_remote_copy(
            src_ref=ksend,
            dst_ref=kgot.at[1 + strip],
            send_sem=kx_sem.at[0],
            recv_sem=kx_sem.at[1],
            device_id=pdev,
            device_id_type=MESH,
        )

    near = [(0, 1, 0), (0, 1, 1), (1, 1, 0), (1, 1, 1)]
    far = [(1, 0, 0), (1, 0, 1)]
    sibling = (0, 0, 1)
    remote = [sibling] + near + far

    build(0)
    inner = jnp.logical_and(has_before, has_after)

    @pl.when(inner)
    def _():
        pl.semaphore_wait(barrier, 9)

    @pl.when(jnp.logical_not(inner))
    def _():
        pl.semaphore_wait(barrier, 8 if pairs > 1 else 7)

    start = lambda cp: cp.start()
    k_copy(lo).start()
    for o in remote:
        x_copy(0, o).start()
    own_copy(0).start()
    build(1)
    own_copy(0).wait()
    forward(0, (0, 0, 0), start)
    own_copy(1).start()

    highest = lax.Precision.HIGHEST
    mats[0, :, 0:LEVELS] = thermal_ref[...]
    mats[1, :, 0:LEVELS] = water_ref[...]
    mats[0, :, LEVELS:] = -0.25 * jnp.dot(thermal_ref[...], deriv_ref[...], precision=highest, preferred_element_type=jnp.float32)
    mats[1, :, LEVELS:] = 0.5 * jnp.dot(water_ref[...], deriv_ref[...], precision=highest, preferred_element_type=jnp.float32)

    k_copy(1 - lo).wait_recv()
    k_forward(0, start)
    k_forward(1, start)

    def arrive(k, o):
        x_arrival(k, o).wait_recv()
        forward(k, o, start)

    arrive(0, sibling)
    own_copy(1).wait()

    def k_received():
        @pl.when(has_after)
        def _():
            pltpu.make_async_remote_copy(
                src_ref=kgot.at[1], dst_ref=kgot.at[3], send_sem=kz_sem.at[0], recv_sem=kzrecv.at[0],
                device_id=(my_lat - 2, my_d), device_id_type=MESH,
            ).wait_recv()

        @pl.when(has_before)
        def _():
            pltpu.make_async_remote_copy(
                src_ref=kgot.at[2], dst_ref=kgot.at[0], send_sem=kz_sem.at[1], recv_sem=kzrecv.at[1],
                device_id=(my_lat + 2, my_d), device_id_type=MESH,
            ).wait_recv()

        for k in range(CHUNKS):
            for r in range(16):
                for part in range(2):
                    cols = slice(part * LANES, (part + 1) * LANES)
                    kh = jnp.broadcast_to(kgot[r // 4, k, part, r % 4:r % 4 + 1, :], (8, LANES))
                    km = jnp.broadcast_to(kgot[r // 4, k, part, 4 + r % 4:5 + r % 4, :], (8, LANES))
                    coef[k, 0, r, :, cols] = 0.375 * kh
                    coef[k, 1, r, :, cols] = 0.125 * kh
                    coef[k, 2, r, :, cols] = 0.25 * km
                    if part == 0 and 4 <= r < 12:
                        half = slice(((r - 4) % 2) * LANES, ((r - 4) % 2 + 1) * LANES)
                        kmid[k, (r - 4) // 2, :, half] = km

    inside = jnp.logical_or(right, left)

    def stencil(k, q):
        d = flip(hi, q // 2) * 2 + flip(core, q % 2)

        @pl.loop(0, 4)
        def _(tile):
            level = pl.multiple_of(d * SLAB + tile * 8, 8)

            def load(r, f):
                row = r % 4
                main = piece[k, r // 4, q, pl.ds(pl.multiple_of((f * 16 + row * 4 + tile) * 8, 8), 8), :]
                packed = piece[k, r // 4, q, pl.ds(256 + f * 8, 8), :]
                shift = lax.rem(LANES - 8 * (row * 4 + tile), LANES)
                edge = jnp.where(inside, pltpu.roll(packed, shift, 1), 0.0)
                return jnp.concatenate([main, edge], axis=1)

            def lap(rows, r):
                centre = rows[r]
                east = pltpu.roll(centre, 2 * LANES - 1, 1)
                west = pltpu.roll(centre, 1, 1)
                return rows[r + 1] + rows[r - 1] + east + west - 4.0 * centre

            heat = [{} for _ in range(LSUB + 1)]
            wet = [{} for _ in range(LSUB + 1)]
            for front in range(16):
                heat[0][front] = load(front, 0)
                wet[0][front] = load(front, 1)
                for t in range(1, LSUB + 1):
                    r = front - t
                    if r < t or r > 15 - t:
                        continue
                    h, w = heat[t - 1][r], wet[t - 1][r]
                    factor = coef[k, 0, r] - coef[k, 1, r] / (1.0 + w * w)
                    heat[t][r] = h + factor * lap(heat[t - 1], r)
                    wet[t][r] = w + coef[k, 2, r] * lap(wet[t - 1], r)
                    if t == LSUB:
                        half = slice(((r - 4) % 2) * LANES, ((r - 4) % 2 + 1) * LANES)
                        state[k, 0, (r - 4) // 2, pl.ds(level, 8), half] = heat[t][r][:, :LANES]
                        state[k, 1, (r - 4) // 2, pl.ds(level, 8), half] = wet[t][r][:, :LANES]

    def r_copy(k, half, o):
        lo2, d2, dev = place(o)
        n = OFFSETS.index(o)
        return pltpu.make_async_remote_copy(
            src_ref=solved.at[k, :, pl.ds(lo2 * 4 + half * 2, 2), pl.ds(pl.multiple_of(d2 * SLAB, SLAB), SLAB), :],
            dst_ref=result.at[:, pl.ds(half * 2, 2), :, pl.ds(pl.multiple_of((k * 8 + me) * LANES, LANES), LANES)],
            send_sem=rsend.at[k, half, n],
            recv_sem=rrecv.at[k, half, n],
            device_id=dev,
            device_id_type=MESH,
        )

    def r_arrival(k, half, o):
        lo2, d2, dev = place(o)
        n = OFFSETS.index(o)
        src = (k * 8 + lo2 * 4 + d2) * LANES
        return pltpu.make_async_remote_copy(
            src_ref=solved.at[k, :, pl.ds(lo2 * 4 + half * 2, 2), pl.ds(pl.multiple_of(d2 * SLAB, SLAB), SLAB), :],
            dst_ref=result.at[:, pl.ds(half * 2, 2), :, pl.ds(pl.multiple_of(src, LANES), LANES)],
            send_sem=rsend.at[k, half, n],
            recv_sem=rrecv.at[k, half, n],
            device_id=dev,
            device_id_type=MESH,
        )

    def r_own(k, half):
        return pltpu.make_async_copy(
            solved.at[k, :, pl.ds(lo * 4 + half * 2, 2), pl.ds(pl.multiple_of(my_d * SLAB, SLAB), SLAB), :],
            result.at[:, pl.ds(half * 2, 2), :, pl.ds(pl.multiple_of((k * 8 + me) * LANES, LANES), LANES)],
            rown_sem.at[k, half],
        )

    def solve(k):
        for half in range(2):
            for l in (1, 0):
                rp = flip(lo, l) * 2 + half
                h = state[k, 0, rp]
                w = state[k, 1, rp]
                kw = w * kmid[k, rp, 0:1, :]
                temp = jnp.dot(mats[0], jnp.concatenate([h, kw], axis=0), precision=highest, preferred_element_type=jnp.float32)
                moist = jnp.dot(mats[1], jnp.concatenate([w, kw], axis=0), precision=highest, preferred_element_type=jnp.float32)
                for f, out in enumerate((temp, moist)):
                    solved[k, f, rp * 2] = out[:, :LANES]
                    solved[k, f, rp * 2 + 1] = out[:, LANES:]
                for o in [(1, l, 0), (1, l, 1), (0, l, 0), (0, l, 1)]:
                    if o == (0, 0, 0):
                        r_own(k, half).start()
                    else:
                        r_copy(k, half, o).start()

    for o in near:
        arrive(0, o)
    for o in far:
        arrive(0, o)
    for o in remote:
        x_copy(1, o).start()
    forward(1, (0, 0, 0), start)
    k_received()
    arrive(1, sibling)
    halo_wait(0, 0)
    stencil(0, 0)
    halo_wait(0, 1)
    stencil(0, 1)
    halo_wait(0, 2)
    stencil(0, 2)
    for o in near:
        arrive(1, o)
    halo_wait(0, 3)
    stencil(0, 3)
    solve(0)
    for o in far:
        arrive(1, o)
    for q in range(4):
        halo_wait(1, q)
        stencil(1, q)
    solve(1)

    def store(k):
        cols = pl.ds(k * 8 * LANES, 8 * LANES)
        copies = []
        for f, out in enumerate((heat_out, wet_out)):
            for r in range(4):
                copies.append(pltpu.make_async_copy(result.at[f, r, :, cols], out.at[:, r, cols], store_sem.at[k, f * 4 + r]))
        return copies

    for k in range(CHUNKS):
        for half in range(2):
            r_own(k, half).wait()
            for o in remote:
                r_arrival(k, half, o).wait_recv()
        for cp in store(k):
            cp.start()

    k_copy(lo).wait_send()
    k_forward(0, lambda cp: cp.wait_send())
    k_forward(1, lambda cp: cp.wait_send())
    for k in range(CHUNKS):
        for o in remote:
            x_copy(k, o).wait_send()
        for o in OFFSETS:
            forward(k, o, lambda cp: cp.wait_send())
        for half in range(2):
            for o in remote:
                r_copy(k, half, o).wait_send()
        for cp in store(k):
            cp.wait()


def solution(mesh):
    pairs = mesh.shape["lat"] // 2
    deriv = scaled_derivative()

    def per_device(heat, wet, label, spread, factor, thermal, water):
        any_spec = pl.BlockSpec(memory_space=pl.ANY)
        vmem = pl.BlockSpec(memory_space=pltpu.VMEM)
        smem = pl.BlockSpec(memory_space=pltpu.SMEM)
        dma = pltpu.SemaphoreType.DMA
        f32 = jnp.float32
        out = jax.ShapeDtypeStruct(heat.shape, f32)
        return pl.pallas_call(
            functools.partial(kernel, pairs),
            out_shape=(out, out),
            in_specs=[any_spec, any_spec, vmem, smem, smem, vmem, vmem, vmem],
            out_specs=(any_spec, any_spec),
            scratch_shapes=[
                pltpu.VMEM((2, 4, SLAB, 16 * LANES), f32),
                pltpu.VMEM((16, PIECE, LANES), f32),
                pltpu.VMEM((CHUNKS, 4, 4, PIECE, LANES), f32),
                pltpu.VMEM((18, 8, LANES), f32),
                pltpu.VMEM((CHUNKS, 2, 8, LANES), f32),
                pltpu.VMEM((4, CHUNKS, 2, 8, LANES), f32),
                pltpu.VMEM((CHUNKS, 3, 16, 8, 2 * LANES), f32),
                pltpu.VMEM((CHUNKS, 4, 8, 2 * LANES), f32),
                pltpu.VMEM((CHUNKS, 2, 4, LEVELS, 2 * LANES), f32),
                pltpu.VMEM((CHUNKS, 2, 8, LEVELS, LANES), f32),
                pltpu.VMEM((2, 4, SLAB, 16 * LANES), f32),
                pltpu.VMEM((2, LEVELS, 2 * LEVELS), f32),
                dma((8,)),
                dma((CHUNKS,)),
                dma((CHUNKS, 8)),
                dma((CHUNKS, 8)),
                dma((CHUNKS, 8)),
                dma((CHUNKS, 4, 2)),
                dma((1,)),
                dma((2,)),
                dma((2,)),
                dma((2,)),
                dma((CHUNKS, 2)),
                dma((CHUNKS, 2, 8)),
                dma((CHUNKS, 2, 8)),
                dma((CHUNKS, 8)),
            ],
            compiler_params=pltpu.CompilerParams(
                collective_id=0, has_side_effects=True, vmem_limit_bytes=48 << 20
            ),
        )(heat, wet, label, spread, factor, thermal, water, jnp.asarray(deriv))

    return jax.shard_map(
        per_device,
        mesh=mesh,
        in_specs=(
            P("depth", "lat", None),
            P("depth", "lat", None),
            P("lat", None),
            P(),
            P(),
            P(),
            P(),
        ),
        out_specs=(P("depth", "lat", None), P("depth", "lat", None)),
        check_vma=False,
    )
```

```python
import functools

import jax
import jax.numpy as jnp
import numpy as np
from jax import lax
from jax.experimental import pallas as pl
from jax.experimental.pallas import tpu as pltpu
from jax.sharding import PartitionSpec as P

MESH = pl.DeviceIdType.MESH
LEVELS = 128
CLASSES = 12
LSUB = 4
CHUNKS = 2
LANES = 128
SLAB = 32
PIECE = 272
OFFSETS = [(h, l, c) for h in (0, 1) for l in (0, 1) for c in (0, 1)]


def scaled_derivative():
    f32 = np.float32
    index = np.arange(LEVELS).astype(f32)
    nodes = np.cos(f32(np.pi) * index / f32(LEVELS - 1)).astype(f32)
    ends = np.where((index == 0) | (index == LEVELS - 1), 2.0, 1.0)
    signs = np.where(np.arange(LEVELS) % 2 == 0, 1.0, -1.0)
    weight = (ends * signs).astype(f32)
    diagonal = np.eye(LEVELS, dtype=bool)
    spread = nodes[:, None] - nodes[None, :]
    off = weight[:, None] / weight[None, :] / np.where(diagonal, f32(1), spread)
    off = np.where(diagonal, f32(0), off)
    deriv = off - np.diag(np.sum(off, axis=1))
    scale = (f32(1) - nodes * nodes) / f32(LEVELS)
    return (scale[:, None] * deriv).astype(f32)


def flip(value, bit):
    return 1 - value if bit else value


def kernel(
    pairs,
    heat_ref, wet_ref, label_ref, spread_ref, factor_ref, thermal_ref, water_ref, deriv_ref,
    heat_out, wet_out,
    slab, block, piece, kloc, ksend, kgot, coef, kmid, state, solved, result, mats,
    load_sem, own_sem, xsend, xrecv, zsend, zrecv, kown_sem, kx_sem, kz_sem, kzrecv, rown_sem, rsend, rrecv, store_sem,
):
    my_lat = lax.axis_index("lat")
    my_d = lax.axis_index("depth")
    pair, lo = my_lat // 2, my_lat % 2
    hi, core = my_d // 2, my_d % 2
    me = lo * 4 + my_d
    has_before, has_after = pair > 0, pair < pairs - 1

    def place(o):
        h, l, c = o
        lo2 = flip(lo, l)
        d2 = flip(hi, h) * 2 + flip(core, c)
        return lo2, d2, (pair * 2 + lo2, d2)

    loads = []
    for f, src in enumerate((heat_ref, wet_ref)):
        for r in range(4):
            loads.append(pltpu.make_async_copy(src.at[:, r, :], slab.at[f, r], load_sem.at[f * 4 + r]))
    for cp in loads:
        cp.start()

    barrier = pltpu.get_barrier_semaphore()
    for o in OFFSETS[1:]:
        pl.semaphore_signal(barrier, inc=1, device_id=place(o)[2], device_id_type=MESH)

    @pl.when(has_before)
    def _():
        pl.semaphore_signal(barrier, inc=1, device_id=(my_lat - 2, my_d), device_id_type=MESH)

    @pl.when(has_after)
    def _():
        pl.semaphore_signal(barrier, inc=1, device_id=(my_lat + 2, my_d), device_id_type=MESH)

    lane = lax.broadcasted_iota(jnp.int32, (8, LANES), 1)
    right, left = lane < 4, lane >= LANES - 4

    kloc[0] = jnp.zeros((8, LANES), jnp.float32)
    kloc[17] = jnp.zeros((8, LANES), jnp.float32)
    for t in range(16):
        label = label_ref[:, t * LANES:(t + 1) * LANES]
        kh = jnp.zeros((4, LANES), jnp.float32)
        km = jnp.zeros((4, LANES), jnp.float32)
        for n in range(CLASSES):
            kh = jnp.where(label == n, spread_ref[n], kh)
            km = jnp.where(label == n, factor_ref[n], km)
        kloc[t + 1, 0:4] = kh
        kloc[t + 1, 4:8] = km

    def kblock(t):
        main = kloc[t + 1]
        edge = jnp.where(right, kloc[t + 2], jnp.where(left, kloc[t], 0.0))
        return main, edge

    partner = (0, 1, 0)
    plo, pd, pdev = place(partner)
    for k in range(CHUNKS):
        main, edge = kblock(k * 8 + plo * 4 + pd)
        ksend[k, 0] = main
        ksend[k, 1] = edge
        main, edge = kblock(k * 8 + me)
        kgot[1 + lo, k, 0] = main
        kgot[1 + lo, k, 1] = edge

    @pl.when(jnp.logical_not(has_before))
    def _():
        kgot[0] = jnp.zeros((CHUNKS, 2, 8, LANES), jnp.float32)

        @pl.loop(0, CHUNKS * 4)
        def _(i):
            piece[i // 4, 0, i % 4] = jnp.zeros((PIECE, LANES), jnp.float32)

    @pl.when(jnp.logical_not(has_after))
    def _():
        kgot[3] = jnp.zeros((CHUNKS, 2, 8, LANES), jnp.float32)

        @pl.loop(0, CHUNKS * 4)
        def _(i):
            piece[i // 4, 3, i % 4] = jnp.zeros((PIECE, LANES), jnp.float32)

    for cp in loads:
        cp.wait()

    def build(k):
        @pl.loop(0, 8)
        def _(j):
            t = k * 8 + j
            here = pl.multiple_of(t * LANES, LANES)
            before = pl.multiple_of(jnp.maximum(t - 1, 0) * LANES, LANES)
            after = pl.multiple_of(jnp.minimum(t + 1, 15) * LANES, LANES)
            keep_left = jnp.logical_and(left, t > 0)
            keep_right = jnp.logical_and(right, t < 15)
            for f in range(2):
                packed = jnp.zeros((8, LANES), jnp.float32)
                for r in range(4):
                    for q in range(4):
                        g = r * 4 + q
                        rows = pl.ds(q * 8, 8)
                        block[t, pl.ds((f * 16 + g) * 8, 8), :] = slab[f, r, rows, pl.ds(here, LANES)]
                        edge = jnp.where(
                            keep_right,
                            slab[f, r, rows, pl.ds(after, LANES)],
                            jnp.where(keep_left, slab[f, r, rows, pl.ds(before, LANES)], 0.0),
                        )
                        packed = packed + (pltpu.roll(edge, 8 * g, 1) if g else edge)
                block[t, pl.ds(256 + f * 8, 8), :] = packed

    def x_copy(k, o):
        lo2, d2, dev = place(o)
        n = OFFSETS.index(o)
        return pltpu.make_async_remote_copy(
            src_ref=block.at[k * 8 + lo2 * 4 + d2],
            dst_ref=piece.at[k, 1 + lo, o[0] * 2 + o[2]],
            send_sem=xsend.at[k, n],
            recv_sem=xrecv.at[k, n],
            device_id=dev,
            device_id_type=MESH,
        )

    def x_arrival(k, o):
        lo2, d2, dev = place(o)
        n = OFFSETS.index(o)
        return pltpu.make_async_remote_copy(
            src_ref=block.at[k * 8 + lo2 * 4 + d2],
            dst_ref=piece.at[k, 1 + lo2, o[0] * 2 + o[2]],
            send_sem=xsend.at[k, n],
            recv_sem=xrecv.at[k, n],
            device_id=dev,
            device_id_type=MESH,
        )

    def own_copy(k):
        return pltpu.make_async_copy(block.at[k * 8 + me], piece.at[k, 1 + lo, 0], own_sem.at[k])

    def forward_copy(k, o, s):
        n = OFFSETS.index(o)
        q = o[0] * 2 + o[2]
        return pltpu.make_async_remote_copy(
            src_ref=piece.at[k, 1 + s, q],
            dst_ref=piece.at[k, 3 if s == 0 else 0, q],
            send_sem=zsend.at[k, n],
            recv_sem=zrecv.at[k, q, s],
            device_id=(my_lat - 2 if s == 0 else my_lat + 2, my_d),
            device_id_type=MESH,
        )

    def forward(k, o, act):
        lo2 = flip(lo, o[1])

        @pl.when(jnp.logical_and(lo2 == 0, has_before))
        def _():
            act(forward_copy(k, o, 0))

        @pl.when(jnp.logical_and(lo2 == 1, has_after))
        def _():
            act(forward_copy(k, o, 1))

    def halo_wait(k, q):
        o = (q // 2, 0, q % 2)

        @pl.when(has_after)
        def _():
            forward_copy(k, o, 0).wait_recv()

        @pl.when(has_before)
        def _():
            forward_copy(k, o, 1).wait_recv()

    def k_forward(s, act):
        @pl.when(has_before if s == 0 else has_after)
        def _():
            act(
                pltpu.make_async_remote_copy(
                    src_ref=kgot.at[1 + s],
                    dst_ref=kgot.at[3 if s == 0 else 0],
                    send_sem=kz_sem.at[s],
                    recv_sem=kzrecv.at[s],
                    device_id=(my_lat - 2 if s == 0 else my_lat + 2, my_d),
                    device_id_type=MESH,
                )
            )

    def k_copy(strip):
        return pltpu.make_async_remote_copy(
            src_ref=ksend,
            dst_ref=kgot.at[1 + strip],
            send_sem=kx_sem.at[0],
            recv_sem=kx_sem.at[1],
            device_id=pdev,
            device_id_type=MESH,
        )

    near = [(0, 1, 0), (0, 1, 1), (1, 1, 0), (1, 1, 1)]
    far = [(1, 0, 0), (1, 0, 1)]
    sibling = (0, 0, 1)
    remote = [sibling] + near + far

    build(0)
    inner = jnp.logical_and(has_before, has_after)

    @pl.when(inner)
    def _():
        pl.semaphore_wait(barrier, 9)

    @pl.when(jnp.logical_not(inner))
    def _():
        pl.semaphore_wait(barrier, 8 if pairs > 1 else 7)

    start = lambda cp: cp.start()
    k_copy(lo).start()
    for o in remote:
        x_copy(0, o).start()
    own_copy(0).start()
    build(1)
    own_copy(0).wait()
    forward(0, (0, 0, 0), start)
    own_copy(1).start()

    highest = lax.Precision.HIGHEST
    mats[0, :, 0:LEVELS] = thermal_ref[...]
    mats[1, :, 0:LEVELS] = water_ref[...]
    mats[0, :, LEVELS:] = -0.25 * jnp.dot(thermal_ref[...], deriv_ref[...], precision=highest, preferred_element_type=jnp.float32)
    mats[1, :, LEVELS:] = 0.5 * jnp.dot(water_ref[...], deriv_ref[...], precision=highest, preferred_element_type=jnp.float32)

    k_copy(1 - lo).wait_recv()
    k_forward(0, start)
    k_forward(1, start)

    def arrive(k, o):
        x_arrival(k, o).wait_recv()
        forward(k, o, start)

    arrive(0, sibling)
    own_copy(1).wait()

    def k_received():
        @pl.when(has_after)
        def _():
            pltpu.make_async_remote_copy(
                src_ref=kgot.at[1], dst_ref=kgot.at[3], send_sem=kz_sem.at[0], recv_sem=kzrecv.at[0],
                device_id=(my_lat - 2, my_d), device_id_type=MESH,
            ).wait_recv()

        @pl.when(has_before)
        def _():
            pltpu.make_async_remote_copy(
                src_ref=kgot.at[2], dst_ref=kgot.at[0], send_sem=kz_sem.at[1], recv_sem=kzrecv.at[1],
                device_id=(my_lat + 2, my_d), device_id_type=MESH,
            ).wait_recv()

        for k in range(CHUNKS):
            for r in range(16):
                for part in range(2):
                    cols = slice(part * LANES, (part + 1) * LANES)
                    kh = jnp.broadcast_to(kgot[r // 4, k, part, r % 4:r % 4 + 1, :], (8, LANES))
                    km = jnp.broadcast_to(kgot[r // 4, k, part, 4 + r % 4:5 + r % 4, :], (8, LANES))
                    coef[k, 0, r, :, cols] = 0.375 * kh
                    coef[k, 1, r, :, cols] = 0.125 * kh
                    coef[k, 2, r, :, cols] = 0.25 * km
                    if part == 0 and 4 <= r < 12:
                        half = slice(((r - 4) % 2) * LANES, ((r - 4) % 2 + 1) * LANES)
                        kmid[k, (r - 4) // 2, :, half] = km

    inside = jnp.logical_or(right, left)

    def stencil(k, q):
        d = flip(hi, q // 2) * 2 + flip(core, q % 2)

        @pl.loop(0, 4)
        def _(tile):
            level = pl.multiple_of(d * SLAB + tile * 8, 8)

            def load(r, f):
                row = r % 4
                main = piece[k, r // 4, q, pl.ds(pl.multiple_of((f * 16 + row * 4 + tile) * 8, 8), 8), :]
                packed = piece[k, r // 4, q, pl.ds(256 + f * 8, 8), :]
                shift = lax.rem(LANES - 8 * (row * 4 + tile), LANES)
                edge = jnp.where(inside, pltpu.roll(packed, shift, 1), 0.0)
                return jnp.concatenate([main, edge], axis=1)

            def lap(rows, r):
                centre = rows[r]
                east = pltpu.roll(centre, 2 * LANES - 1, 1)
                west = pltpu.roll(centre, 1, 1)
                return rows[r + 1] + rows[r - 1] + east + west - 4.0 * centre

            heat = [{} for _ in range(LSUB + 1)]
            wet = [{} for _ in range(LSUB + 1)]
            for front in range(16):
                heat[0][front] = load(front, 0)
                wet[0][front] = load(front, 1)
                for t in range(1, LSUB + 1):
                    r = front - t
                    if r < t or r > 15 - t:
                        continue
                    h, w = heat[t - 1][r], wet[t - 1][r]
                    factor = coef[k, 0, r] - coef[k, 1, r] / (1.0 + w * w)
                    heat[t][r] = h + factor * lap(heat[t - 1], r)
                    wet[t][r] = w + coef[k, 2, r] * lap(wet[t - 1], r)
                    if t == LSUB:
                        half = slice(((r - 4) % 2) * LANES, ((r - 4) % 2 + 1) * LANES)
                        state[k, 0, (r - 4) // 2, pl.ds(level, 8), half] = heat[t][r][:, :LANES]
                        state[k, 1, (r - 4) // 2, pl.ds(level, 8), half] = wet[t][r][:, :LANES]

    def r_copy(k, half, o):
        lo2, d2, dev = place(o)
        n = OFFSETS.index(o)
        return pltpu.make_async_remote_copy(
            src_ref=solved.at[k, :, pl.ds(lo2 * 4 + half * 2, 2), pl.ds(pl.multiple_of(d2 * SLAB, SLAB), SLAB), :],
            dst_ref=result.at[:, pl.ds(half * 2, 2), :, pl.ds(pl.multiple_of((k * 8 + me) * LANES, LANES), LANES)],
            send_sem=rsend.at[k, half, n],
            recv_sem=rrecv.at[k, half, n],
            device_id=dev,
            device_id_type=MESH,
        )

    def r_arrival(k, half, o):
        lo2, d2, dev = place(o)
        n = OFFSETS.index(o)
        src = (k * 8 + lo2 * 4 + d2) * LANES
        return pltpu.make_async_remote_copy(
            src_ref=solved.at[k, :, pl.ds(lo2 * 4 + half * 2, 2), pl.ds(pl.multiple_of(d2 * SLAB, SLAB), SLAB), :],
            dst_ref=result.at[:, pl.ds(half * 2, 2), :, pl.ds(pl.multiple_of(src, LANES), LANES)],
            send_sem=rsend.at[k, half, n],
            recv_sem=rrecv.at[k, half, n],
            device_id=dev,
            device_id_type=MESH,
        )

    def r_own(k, half):
        return pltpu.make_async_copy(
            solved.at[k, :, pl.ds(lo * 4 + half * 2, 2), pl.ds(pl.multiple_of(my_d * SLAB, SLAB), SLAB), :],
            result.at[:, pl.ds(half * 2, 2), :, pl.ds(pl.multiple_of((k * 8 + me) * LANES, LANES), LANES)],
            rown_sem.at[k, half],
        )

    def solve(k):
        for half in range(2):
            for l in (1, 0):
                rp = flip(lo, l) * 2 + half
                h = state[k, 0, rp]
                w = state[k, 1, rp]
                kw = w * kmid[k, rp, 0:1, :]
                temp = jnp.dot(mats[0], jnp.concatenate([h, kw], axis=0), precision=highest, preferred_element_type=jnp.float32)
                moist = jnp.dot(mats[1], jnp.concatenate([w, kw], axis=0), precision=highest, preferred_element_type=jnp.float32)
                for f, out in enumerate((temp, moist)):
                    solved[k, f, rp * 2] = out[:, :LANES]
                    solved[k, f, rp * 2 + 1] = out[:, LANES:]
                for o in [(1, l, 0), (1, l, 1), (0, l, 0), (0, l, 1)]:
                    if o == (0, 0, 0):
                        r_own(k, half).start()
                    else:
                        r_copy(k, half, o).start()

    for o in near:
        arrive(0, o)
    for o in remote:
        x_copy(1, o).start()
    forward(1, (0, 0, 0), start)
    for o in far:
        arrive(0, o)
    k_received()
    arrive(1, sibling)
    halo_wait(0, 0)
    stencil(0, 0)
    halo_wait(0, 1)
    stencil(0, 1)
    halo_wait(0, 2)
    stencil(0, 2)
    for o in near:
        arrive(1, o)
    halo_wait(0, 3)
    stencil(0, 3)
    solve(0)
    for o in far:
        arrive(1, o)
    for q in range(4):
        halo_wait(1, q)
        stencil(1, q)
    solve(1)

    def store(k):
        cols = pl.ds(k * 8 * LANES, 8 * LANES)
        copies = []
        for f, out in enumerate((heat_out, wet_out)):
            for r in range(4):
                copies.append(pltpu.make_async_copy(result.at[f, r, :, cols], out.at[:, r, cols], store_sem.at[k, f * 4 + r]))
        return copies

    for k in range(CHUNKS):
        for half in range(2):
            r_own(k, half).wait()
            for o in remote:
                r_arrival(k, half, o).wait_recv()
        for cp in store(k):
            cp.start()

    k_copy(lo).wait_send()
    k_forward(0, lambda cp: cp.wait_send())
    k_forward(1, lambda cp: cp.wait_send())
    for k in range(CHUNKS):
        for o in remote:
            x_copy(k, o).wait_send()
        for o in OFFSETS:
            forward(k, o, lambda cp: cp.wait_send())
        for half in range(2):
            for o in remote:
                r_copy(k, half, o).wait_send()
        for cp in store(k):
            cp.wait()


def solution(mesh):
    pairs = mesh.shape["lat"] // 2
    deriv = scaled_derivative()

    def per_device(heat, wet, label, spread, factor, thermal, water):
        any_spec = pl.BlockSpec(memory_space=pl.ANY)
        vmem = pl.BlockSpec(memory_space=pltpu.VMEM)
        smem = pl.BlockSpec(memory_space=pltpu.SMEM)
        dma = pltpu.SemaphoreType.DMA
        f32 = jnp.float32
        out = jax.ShapeDtypeStruct(heat.shape, f32)
        return pl.pallas_call(
            functools.partial(kernel, pairs),
            out_shape=(out, out),
            in_specs=[any_spec, any_spec, vmem, smem, smem, vmem, vmem, vmem],
            out_specs=(any_spec, any_spec),
            scratch_shapes=[
                pltpu.VMEM((2, 4, SLAB, 16 * LANES), f32),
                pltpu.VMEM((16, PIECE, LANES), f32),
                pltpu.VMEM((CHUNKS, 4, 4, PIECE, LANES), f32),
                pltpu.VMEM((18, 8, LANES), f32),
                pltpu.VMEM((CHUNKS, 2, 8, LANES), f32),
                pltpu.VMEM((4, CHUNKS, 2, 8, LANES), f32),
                pltpu.VMEM((CHUNKS, 3, 16, 8, 2 * LANES), f32),
                pltpu.VMEM((CHUNKS, 4, 8, 2 * LANES), f32),
                pltpu.VMEM((CHUNKS, 2, 4, LEVELS, 2 * LANES), f32),
                pltpu.VMEM((CHUNKS, 2, 8, LEVELS, LANES), f32),
                pltpu.VMEM((2, 4, SLAB, 16 * LANES), f32),
                pltpu.VMEM((2, LEVELS, 2 * LEVELS), f32),
                dma((8,)),
                dma((CHUNKS,)),
                dma((CHUNKS, 8)),
                dma((CHUNKS, 8)),
                dma((CHUNKS, 8)),
                dma((CHUNKS, 4, 2)),
                dma((1,)),
                dma((2,)),
                dma((2,)),
                dma((2,)),
                dma((CHUNKS, 2)),
                dma((CHUNKS, 2, 8)),
                dma((CHUNKS, 2, 8)),
                dma((CHUNKS, 8)),
            ],
            compiler_params=pltpu.CompilerParams(
                collective_id=0, has_side_effects=True, vmem_limit_bytes=48 << 20
            ),
        )(*(pltpu.with_memory_space_constraint(x, pltpu.HBM) for x in (heat, wet, label, spread, factor, thermal, water, jnp.asarray(deriv))))

    return jax.shard_map(
        per_device,
        mesh=mesh,
        in_specs=(
            P("depth", "lat", None),
            P("depth", "lat", None),
            P("lat", None),
            P(),
            P(),
            P(),
            P(),
        ),
        out_specs=(P("depth", "lat", None), P("depth", "lat", None)),
        check_vma=False,
    )
```

```python
import functools

import jax
import jax.numpy as jnp
import numpy as np
from jax import lax
from jax.experimental import pallas as pl
from jax.experimental.pallas import tpu as pltpu
from jax.sharding import PartitionSpec as P

MESH = pl.DeviceIdType.MESH
LEVELS = 128
CLASSES = 12
LSUB = 4
CHUNKS = 2
LANES = 128
SLAB = 32
PIECE = 272
FIRST, LAST = 16, 16 + LANES
SPAN = LAST + 16
OFFSETS = [(h, l, c) for h in (0, 1) for l in (0, 1) for c in (0, 1)]


def scaled_derivative():
    f32 = np.float32
    index = np.arange(LEVELS).astype(f32)
    nodes = np.cos(f32(np.pi) * index / f32(LEVELS - 1)).astype(f32)
    ends = np.where((index == 0) | (index == LEVELS - 1), 2.0, 1.0)
    signs = np.where(np.arange(LEVELS) % 2 == 0, 1.0, -1.0)
    weight = (ends * signs).astype(f32)
    diagonal = np.eye(LEVELS, dtype=bool)
    spread = nodes[:, None] - nodes[None, :]
    off = weight[:, None] / weight[None, :] / np.where(diagonal, f32(1), spread)
    off = np.where(diagonal, f32(0), off)
    deriv = off - np.diag(np.sum(off, axis=1))
    scale = (f32(1) - nodes * nodes) / f32(LEVELS)
    return (scale[:, None] * deriv).astype(f32)


def flip(value, bit):
    return 1 - value if bit else value


def kernel(
    pairs,
    heat_ref, wet_ref, label_ref, spread_ref, factor_ref, thermal_ref, water_ref, deriv_ref,
    heat_out, wet_out,
    slab, block, piece, kloc, ksend, kgot, coef, turned, state, solved, result, mats,
    load_sem, own_sem, xsend, xrecv, zsend, zrecv, kown_sem, kx_sem, kz_sem, kzrecv, rown_sem, rsend, rrecv, store_sem,
):
    my_lat = lax.axis_index("lat")
    my_d = lax.axis_index("depth")
    pair, lo = my_lat // 2, my_lat % 2
    hi, core = my_d // 2, my_d % 2
    me = lo * 4 + my_d
    has_before, has_after = pair > 0, pair < pairs - 1

    def place(o):
        h, l, c = o
        lo2 = flip(lo, l)
        d2 = flip(hi, h) * 2 + flip(core, c)
        return lo2, d2, (pair * 2 + lo2, d2)

    loads = []
    for f, src in enumerate((heat_ref, wet_ref)):
        for r in range(4):
            loads.append(pltpu.make_async_copy(src.at[:, r, :], slab.at[f, r], load_sem.at[f * 4 + r]))
    for cp in loads:
        cp.start()

    barrier = pltpu.get_barrier_semaphore()
    for o in OFFSETS[1:]:
        pl.semaphore_signal(barrier, inc=1, device_id=place(o)[2], device_id_type=MESH)

    @pl.when(has_before)
    def _():
        pl.semaphore_signal(barrier, inc=1, device_id=(my_lat - 2, my_d), device_id_type=MESH)

    @pl.when(has_after)
    def _():
        pl.semaphore_signal(barrier, inc=1, device_id=(my_lat + 2, my_d), device_id_type=MESH)

    lane = lax.broadcasted_iota(jnp.int32, (8, LANES), 1)
    right, left = lane < 4, lane >= LANES - 4

    kloc[0] = jnp.zeros((8, LANES), jnp.float32)
    kloc[17] = jnp.zeros((8, LANES), jnp.float32)
    for t in range(16):
        label = label_ref[:, t * LANES:(t + 1) * LANES]
        kh = jnp.zeros((4, LANES), jnp.float32)
        km = jnp.zeros((4, LANES), jnp.float32)
        for n in range(CLASSES):
            kh = jnp.where(label == n, spread_ref[n], kh)
            km = jnp.where(label == n, factor_ref[n], km)
        kloc[t + 1, 0:4] = kh
        kloc[t + 1, 4:8] = km

    def kblock(t):
        main = kloc[t + 1]
        edge = jnp.where(right, kloc[t + 2], jnp.where(left, kloc[t], 0.0))
        return main, edge

    partner = (0, 1, 0)
    plo, pd, pdev = place(partner)
    for k in range(CHUNKS):
        main, edge = kblock(k * 8 + plo * 4 + pd)
        ksend[k, 0] = main
        ksend[k, 1] = edge
        main, edge = kblock(k * 8 + me)
        kgot[1 + lo, k, 0] = main
        kgot[1 + lo, k, 1] = edge

    @pl.when(jnp.logical_not(has_before))
    def _():
        kgot[0] = jnp.zeros((CHUNKS, 2, 8, LANES), jnp.float32)

        @pl.loop(0, CHUNKS * 4)
        def _(i):
            piece[i // 4, 0, i % 4] = jnp.zeros((PIECE, LANES), jnp.float32)

    @pl.when(jnp.logical_not(has_after))
    def _():
        kgot[3] = jnp.zeros((CHUNKS, 2, 8, LANES), jnp.float32)

        @pl.loop(0, CHUNKS * 4)
        def _(i):
            piece[i // 4, 3, i % 4] = jnp.zeros((PIECE, LANES), jnp.float32)

    for cp in loads:
        cp.wait()

    def build(k):
        @pl.loop(0, 8)
        def _(j):
            t = k * 8 + j
            here = pl.multiple_of(t * LANES, LANES)
            before = pl.multiple_of(jnp.maximum(t - 1, 0) * LANES, LANES)
            after = pl.multiple_of(jnp.minimum(t + 1, 15) * LANES, LANES)
            keep_left = jnp.logical_and(left, t > 0)
            keep_right = jnp.logical_and(right, t < 15)
            for f in range(2):
                packed = jnp.zeros((8, LANES), jnp.float32)
                for r in range(4):
                    for q in range(4):
                        g = q * 4 + r
                        rows = pl.ds(q * 8, 8)
                        block[t, pl.ds((f * 16 + r * 4 + q) * 8, 8), :] = slab[f, r, rows, pl.ds(here, LANES)]
                        edge = jnp.where(
                            keep_right,
                            slab[f, r, rows, pl.ds(after, LANES)],
                            jnp.where(keep_left, slab[f, r, rows, pl.ds(before, LANES)], 0.0),
                        )
                        packed = packed + (pltpu.roll(edge, 8 * g, 1) if g else edge)
                block[t, pl.ds(256 + f * 8, 8), :] = packed

    def x_copy(k, o):
        lo2, d2, dev = place(o)
        n = OFFSETS.index(o)
        return pltpu.make_async_remote_copy(
            src_ref=block.at[k * 8 + lo2 * 4 + d2],
            dst_ref=piece.at[k, 1 + lo, o[0] * 2 + o[2]],
            send_sem=xsend.at[k, n],
            recv_sem=xrecv.at[k, n],
            device_id=dev,
            device_id_type=MESH,
        )

    def x_arrival(k, o):
        lo2, d2, dev = place(o)
        n = OFFSETS.index(o)
        return pltpu.make_async_remote_copy(
            src_ref=block.at[k * 8 + lo2 * 4 + d2],
            dst_ref=piece.at[k, 1 + lo2, o[0] * 2 + o[2]],
            send_sem=xsend.at[k, n],
            recv_sem=xrecv.at[k, n],
            device_id=dev,
            device_id_type=MESH,
        )

    def own_copy(k):
        return pltpu.make_async_copy(block.at[k * 8 + me], piece.at[k, 1 + lo, 0], own_sem.at[k])

    def forward_copy(k, o, s):
        n = OFFSETS.index(o)
        q = o[0] * 2 + o[2]
        return pltpu.make_async_remote_copy(
            src_ref=piece.at[k, 1 + s, q],
            dst_ref=piece.at[k, 3 if s == 0 else 0, q],
            send_sem=zsend.at[k, n],
            recv_sem=zrecv.at[k, q, s],
            device_id=(my_lat - 2 if s == 0 else my_lat + 2, my_d),
            device_id_type=MESH,
        )

    def forward(k, o, act):
        lo2 = flip(lo, o[1])

        @pl.when(jnp.logical_and(lo2 == 0, has_before))
        def _():
            act(forward_copy(k, o, 0))

        @pl.when(jnp.logical_and(lo2 == 1, has_after))
        def _():
            act(forward_copy(k, o, 1))

    def halo_wait(k, q):
        o = (q // 2, 0, q % 2)

        @pl.when(has_after)
        def _():
            forward_copy(k, o, 0).wait_recv()

        @pl.when(has_before)
        def _():
            forward_copy(k, o, 1).wait_recv()

    def k_forward(s, act):
        @pl.when(has_before if s == 0 else has_after)
        def _():
            act(
                pltpu.make_async_remote_copy(
                    src_ref=kgot.at[1 + s],
                    dst_ref=kgot.at[3 if s == 0 else 0],
                    send_sem=kz_sem.at[s],
                    recv_sem=kzrecv.at[s],
                    device_id=(my_lat - 2 if s == 0 else my_lat + 2, my_d),
                    device_id_type=MESH,
                )
            )

    def k_copy(strip):
        return pltpu.make_async_remote_copy(
            src_ref=ksend,
            dst_ref=kgot.at[1 + strip],
            send_sem=kx_sem.at[0],
            recv_sem=kx_sem.at[1],
            device_id=pdev,
            device_id_type=MESH,
        )

    near = [(0, 1, 0), (1, 1, 0), (0, 1, 1), (1, 1, 1)]
    far = [(1, 0, 0), (1, 0, 1)]
    sibling = (0, 0, 1)
    remote = [sibling] + near + far

    build(0)
    inner = jnp.logical_and(has_before, has_after)

    @pl.when(inner)
    def _():
        pl.semaphore_wait(barrier, 9)

    @pl.when(jnp.logical_not(inner))
    def _():
        pl.semaphore_wait(barrier, 8 if pairs > 1 else 7)

    start = lambda cp: cp.start()
    k_copy(lo).start()
    for o in remote:
        x_copy(0, o).start()
    own_copy(0).start()
    own_copy(0).wait()
    forward(0, (0, 0, 0), start)
    build(1)
    own_copy(1).start()
    for o in remote:
        x_copy(1, o).start()

    k_copy(1 - lo).wait_recv()
    k_forward(0, start)
    k_forward(1, start)

    def arrive(k, o):
        x_arrival(k, o).wait_recv()
        forward(k, o, start)

    arrive(0, sibling)
    own_copy(1).wait()

    def k_received():
        @pl.when(has_after)
        def _():
            pltpu.make_async_remote_copy(
                src_ref=kgot.at[1], dst_ref=kgot.at[3], send_sem=kz_sem.at[0], recv_sem=kzrecv.at[0],
                device_id=(my_lat - 2, my_d), device_id_type=MESH,
            ).wait_recv()

        @pl.when(has_before)
        def _():
            pltpu.make_async_remote_copy(
                src_ref=kgot.at[2], dst_ref=kgot.at[0], send_sem=kz_sem.at[1], recv_sem=kzrecv.at[1],
                device_id=(my_lat + 2, my_d), device_id_type=MESH,
            ).wait_recv()

    sub = lax.broadcasted_iota(jnp.int32, (8, LANES), 0)

    def put_edges(edges, dst, row):
        dst[row, FIRST - 8:FIRST] = jnp.where(sub >= 4, edges[(row + 15) % 16 * 8:(row + 15) % 16 * 8 + 8], 0.0)
        dst[row, LAST:LAST + 8] = jnp.where(sub < 4, edges[row * 8:row * 8 + 8], 0.0)

    def diffusivities(k):
        for kind in range(2):
            dst = coef.at[k, kind]

            @pl.loop(0, 16)
            def _(r):
                line = kgot[r // 4, k, 0, pl.ds(kind * 4 + r % 4, 1), :]
                dst[r, FIRST:LAST] = 0.25 * jnp.broadcast_to(line, (LANES, LANES)).T

            edges = jnp.zeros((8, LANES), jnp.float32)
            for r in range(16):
                line = jnp.broadcast_to(kgot[r // 4, k, 1, kind * 4 + r % 4:kind * 4 + r % 4 + 1, :], (8, LANES))
                edges = edges + (pltpu.roll(line, 8 * r, 1) if r else line)
            edges = 0.25 * jnp.broadcast_to(edges[0:1], (LANES, LANES)).T
            for r in range(16):
                put_edges(edges, dst, r)

    def slot(d):
        h2, c2 = d // 2, d % 2
        return ((1 - hi) if h2 else hi) * 2 + ((1 - core) if c2 else core)

    def turn(k, outer):
        slots = [slot(d) for d in range(4)]

        @pl.loop(0, 16)
        def _(i):
            f, r = i // 8, i % 8
            row = (r + r // 4 * 8) if outer else r + 4
            rows = pl.ds(pl.multiple_of(f * 128 + r % 4 * 32, 32), 32)
            levels = jnp.concatenate([piece[k, row // 4, q, rows, :] for q in slots], axis=0)
            turned[0, f, row, FIRST:LAST] = levels.T

        if not outer:
            return

        for f in range(2):
            blocks = []
            for q in slots:
                packs = [piece[k, strip, q, 256 + f * 8:264 + f * 8, :] for strip in range(4)]
                for tile in range(4):
                    total = jnp.zeros((8, LANES), jnp.float32)
                    for strip in range(4):
                        shift = 32 * (strip - tile) % LANES
                        moved = pltpu.roll(packs[strip], shift, 1) if shift else packs[strip]
                        inside = (lane + 4) % LANES // 32 == strip
                        total = jnp.where(inside, moved, total)
                    blocks.append(total)
            edges = jnp.concatenate(blocks, axis=0).T
            for r in range(16):
                put_edges(edges, turned.at[0, f], r)

    def stencil(k):
        for t in range(LSUB):
            src, dst = turned.at[t % 2], turned.at[1 - t % 2]
            last = t == LSUB - 1

            @pl.loop(t + 1, 15 - t)
            def _(r):
                for s in range(FIRST if last else FIRST - 8, LAST if last else LAST + 8, 8):
                    def lap(f, centre):
                        return (
                            src[f, r + 1, s:s + 8] + src[f, r - 1, s:s + 8]
                            + src[f, r, s + 1:s + 9] + src[f, r, s - 1:s + 7] - 4.0 * centre
                        )

                    h, w = src[0, r, s:s + 8], src[1, r, s:s + 8]
                    factor = coef[k, 0, r, s:s + 8] * (1.5 - 0.5 / (1.0 + w * w))
                    h2 = h + factor * lap(0, h)
                    w2 = w + coef[k, 1, r, s:s + 8] * lap(1, w)
                    if last:
                        state[k, 0, r - 4, s - FIRST:s - FIRST + 8] = h2
                        state[k, 1, r - 4, s - FIRST:s - FIRST + 8] = w2
                    else:
                        dst[0, r, s:s + 8] = h2
                        dst[1, r, s:s + 8] = w2

    def r_copy(k, half, o):
        lo2, d2, dev = place(o)
        n = OFFSETS.index(o)
        return pltpu.make_async_remote_copy(
            src_ref=solved.at[k, :, pl.ds(lo2 * 4 + half * 2, 2), pl.ds(pl.multiple_of(d2 * SLAB, SLAB), SLAB), :],
            dst_ref=result.at[:, pl.ds(half * 2, 2), :, pl.ds(pl.multiple_of((k * 8 + me) * LANES, LANES), LANES)],
            send_sem=rsend.at[k, half, n],
            recv_sem=rrecv.at[k, half, n],
            device_id=dev,
            device_id_type=MESH,
        )

    def r_arrival(k, half, o):
        lo2, d2, dev = place(o)
        n = OFFSETS.index(o)
        src = (k * 8 + lo2 * 4 + d2) * LANES
        return pltpu.make_async_remote_copy(
            src_ref=solved.at[k, :, pl.ds(lo2 * 4 + half * 2, 2), pl.ds(pl.multiple_of(d2 * SLAB, SLAB), SLAB), :],
            dst_ref=result.at[:, pl.ds(half * 2, 2), :, pl.ds(pl.multiple_of(src, LANES), LANES)],
            send_sem=rsend.at[k, half, n],
            recv_sem=rrecv.at[k, half, n],
            device_id=dev,
            device_id_type=MESH,
        )

    def r_own(k, half):
        return pltpu.make_async_copy(
            solved.at[k, :, pl.ds(lo * 4 + half * 2, 2), pl.ds(pl.multiple_of(my_d * SLAB, SLAB), SLAB), :],
            result.at[:, pl.ds(half * 2, 2), :, pl.ds(pl.multiple_of((k * 8 + me) * LANES, LANES), LANES)],
            rown_sem.at[k, half],
        )

    def solve(k):
        for half in range(2):
            for l in (1, 0):
                rp = flip(lo, l) * 2 + half
                fields = [[], []]
                for r in range(2):
                    h, w = state[k, 0, rp * 2 + r], state[k, 1, rp * 2 + r]
                    kw = w * coef[k, 1, rp * 2 + r + 4, FIRST:LAST]
                    fields[0].append(jnp.concatenate([h, kw], axis=1))
                    fields[1].append(jnp.concatenate([w, kw], axis=1))
                temp, moist = (
                    lax.dot_general(
                        mats[n], jnp.concatenate(fields[n], axis=0), (((1,), (1,)), ((), ())),
                        precision=highest, preferred_element_type=jnp.float32,
                    )
                    for n in range(2)
                )
                for f, out in enumerate((temp, moist)):
                    solved[k, f, rp * 2] = out[:, :LANES]
                    solved[k, f, rp * 2 + 1] = out[:, LANES:]
                for o in [(1, l, 0), (1, l, 1), (0, l, 0), (0, l, 1)]:
                    if o == (0, 0, 0):
                        r_own(k, half).start()
                    else:
                        r_copy(k, half, o).start()

    k_received()
    arrive(0, near[0])
    arrive(0, near[1])
    diffusivities(0)
    arrive(0, near[2])
    arrive(0, near[3])
    diffusivities(1)
    highest = lax.Precision.HIGHEST
    mats[0, :, 0:LEVELS] = thermal_ref[...]
    mats[1, :, 0:LEVELS] = water_ref[...]
    mats[0, :, LEVELS:] = -1.0 * jnp.dot(thermal_ref[...], deriv_ref[...], precision=highest, preferred_element_type=jnp.float32)
    mats[1, :, LEVELS:] = 2.0 * jnp.dot(water_ref[...], deriv_ref[...], precision=highest, preferred_element_type=jnp.float32)

    for o in far:
        arrive(0, o)
    forward(1, (0, 0, 0), start)
    arrive(1, sibling)
    turn(0, False)
    arrive(1, near[0])
    arrive(1, near[1])
    for q in range(4):
        halo_wait(0, q)
    turn(0, True)
    stencil(0)
    arrive(1, near[2])
    arrive(1, near[3])
    solve(0)
    for o in far:
        arrive(1, o)
    turn(1, False)
    for q in range(4):
        halo_wait(1, q)
    turn(1, True)
    stencil(1)
    solve(1)

    def store(k):
        cols = pl.ds(k * 8 * LANES, 8 * LANES)
        copies = []
        for f, out in enumerate((heat_out, wet_out)):
            for r in range(4):
                copies.append(pltpu.make_async_copy(result.at[f, r, :, cols], out.at[:, r, cols], store_sem.at[k, f * 4 + r]))
        return copies

    for k in range(CHUNKS):
        for half in range(2):
            r_own(k, half).wait()
            for o in remote:
                r_arrival(k, half, o).wait_recv()
        for cp in store(k):
            cp.start()

    k_copy(lo).wait_send()
    k_forward(0, lambda cp: cp.wait_send())
    k_forward(1, lambda cp: cp.wait_send())
    for k in range(CHUNKS):
        for o in remote:
            x_copy(k, o).wait_send()
        for o in OFFSETS:
            forward(k, o, lambda cp: cp.wait_send())
        for half in range(2):
            for o in remote:
                r_copy(k, half, o).wait_send()
        for cp in store(k):
            cp.wait()


def solution(mesh):
    pairs = mesh.shape["lat"] // 2
    deriv = scaled_derivative()

    def per_device(heat, wet, label, spread, factor, thermal, water):
        any_spec = pl.BlockSpec(memory_space=pl.ANY)
        vmem = pl.BlockSpec(memory_space=pltpu.VMEM)
        smem = pl.BlockSpec(memory_space=pltpu.SMEM)
        dma = pltpu.SemaphoreType.DMA
        f32 = jnp.float32
        out = jax.ShapeDtypeStruct(heat.shape, f32)
        return pl.pallas_call(
            functools.partial(kernel, pairs),
            out_shape=(out, out),
            in_specs=[any_spec, any_spec, vmem, smem, smem, vmem, vmem, vmem],
            out_specs=(any_spec, any_spec),
            scratch_shapes=[
                pltpu.VMEM((2, 4, SLAB, 16 * LANES), f32),
                pltpu.VMEM((16, PIECE, LANES), f32),
                pltpu.VMEM((CHUNKS, 4, 4, PIECE, LANES), f32),
                pltpu.VMEM((18, 8, LANES), f32),
                pltpu.VMEM((CHUNKS, 2, 8, LANES), f32),
                pltpu.VMEM((4, CHUNKS, 2, 8, LANES), f32),
                pltpu.VMEM((CHUNKS, 2, 16, SPAN, LANES), f32),
                pltpu.VMEM((2, 2, 16, SPAN, LANES), f32),
                pltpu.VMEM((CHUNKS, 2, 8, LANES, LEVELS), f32),
                pltpu.VMEM((CHUNKS, 2, 8, LEVELS, LANES), f32),
                pltpu.VMEM((2, 4, SLAB, 16 * LANES), f32),
                pltpu.VMEM((2, LEVELS, 2 * LEVELS), f32),
                dma((8,)),
                dma((CHUNKS,)),
                dma((CHUNKS, 8)),
                dma((CHUNKS, 8)),
                dma((CHUNKS, 8)),
                dma((CHUNKS, 4, 2)),
                dma((1,)),
                dma((2,)),
                dma((2,)),
                dma((2,)),
                dma((CHUNKS, 2)),
                dma((CHUNKS, 2, 8)),
                dma((CHUNKS, 2, 8)),
                dma((CHUNKS, 8)),
            ],
            compiler_params=pltpu.CompilerParams(
                collective_id=0, has_side_effects=True, vmem_limit_bytes=48 << 20
            ),
        )(*(pltpu.with_memory_space_constraint(x, pltpu.HBM) for x in (heat, wet, label, spread, factor, thermal, water, jnp.asarray(deriv))))

    return jax.shard_map(
        per_device,
        mesh=mesh,
        in_specs=(
            P("depth", "lat", None),
            P("depth", "lat", None),
            P("lat", None),
            P(),
            P(),
            P(),
            P(),
        ),
        out_specs=(P("depth", "lat", None), P("depth", "lat", None)),
        check_vma=False,
    )
```

```python
import functools

import jax
import jax.numpy as jnp
import numpy as np
from jax import lax
from jax.experimental import pallas as pl
from jax.experimental.pallas import tpu as pltpu
from jax.sharding import PartitionSpec as P

MESH = pl.DeviceIdType.MESH
LEVELS = 128
CLASSES = 12
LSUB = 4
CHUNKS = 2
LANES = 128
SLAB = 32
PIECE = 272
FIRST, LAST = 16, 16 + LANES
SPAN = LAST + 16
OFFSETS = [(h, l, c) for h in (0, 1) for l in (0, 1) for c in (0, 1)]


def scaled_derivative():
    f32 = np.float32
    index = np.arange(LEVELS).astype(f32)
    nodes = np.cos(f32(np.pi) * index / f32(LEVELS - 1)).astype(f32)
    ends = np.where((index == 0) | (index == LEVELS - 1), 2.0, 1.0)
    signs = np.where(np.arange(LEVELS) % 2 == 0, 1.0, -1.0)
    weight = (ends * signs).astype(f32)
    diagonal = np.eye(LEVELS, dtype=bool)
    spread = nodes[:, None] - nodes[None, :]
    off = weight[:, None] / weight[None, :] / np.where(diagonal, f32(1), spread)
    off = np.where(diagonal, f32(0), off)
    deriv = off - np.diag(np.sum(off, axis=1))
    scale = (f32(1) - nodes * nodes) / f32(LEVELS)
    return (scale[:, None] * deriv).astype(f32)


def flip(value, bit):
    return 1 - value if bit else value


def kernel(
    pairs,
    heat_ref, wet_ref, label_ref, spread_ref, factor_ref, thermal_ref, water_ref, deriv_ref,
    heat_out, wet_out,
    slab, block, piece, kloc, ksend, kgot, coef, turned, state, solved, result, mats,
    load_sem, own_sem, xsend, xrecv, zsend, zrecv, kown_sem, kx_sem, kz_sem, kzrecv, rown_sem, rsend, rrecv, store_sem,
):
    my_lat = lax.axis_index("lat")
    my_d = lax.axis_index("depth")
    pair, lo = my_lat // 2, my_lat % 2
    hi, core = my_d // 2, my_d % 2
    me = lo * 4 + my_d
    has_before, has_after = pair > 0, pair < pairs - 1

    def place(o):
        h, l, c = o
        lo2 = flip(lo, l)
        d2 = flip(hi, h) * 2 + flip(core, c)
        return lo2, d2, (pair * 2 + lo2, d2)

    loads = []
    for f, src in enumerate((heat_ref, wet_ref)):
        for r in range(4):
            loads.append(pltpu.make_async_copy(src.at[:, r, :], slab.at[f, r], load_sem.at[f * 4 + r]))
    for cp in loads:
        cp.start()

    barrier = pltpu.get_barrier_semaphore()
    for o in OFFSETS[1:]:
        pl.semaphore_signal(barrier, inc=1, device_id=place(o)[2], device_id_type=MESH)

    @pl.when(has_before)
    def _():
        pl.semaphore_signal(barrier, inc=1, device_id=(my_lat - 2, my_d), device_id_type=MESH)

    @pl.when(has_after)
    def _():
        pl.semaphore_signal(barrier, inc=1, device_id=(my_lat + 2, my_d), device_id_type=MESH)

    lane = lax.broadcasted_iota(jnp.int32, (8, LANES), 1)
    right, left = lane < 4, lane >= LANES - 4

    kloc[0] = jnp.zeros((8, LANES), jnp.float32)
    kloc[17] = jnp.zeros((8, LANES), jnp.float32)
    for t in range(16):
        label = label_ref[:, t * LANES:(t + 1) * LANES]
        kh = jnp.zeros((4, LANES), jnp.float32)
        km = jnp.zeros((4, LANES), jnp.float32)
        for n in range(CLASSES):
            kh = jnp.where(label == n, spread_ref[n], kh)
            km = jnp.where(label == n, factor_ref[n], km)
        kloc[t + 1, 0:4] = kh
        kloc[t + 1, 4:8] = km

    def kblock(t):
        main = kloc[t + 1]
        edge = jnp.where(right, kloc[t + 2], jnp.where(left, kloc[t], 0.0))
        return main, edge

    partner = (0, 1, 0)
    plo, pd, pdev = place(partner)
    for k in range(CHUNKS):
        main, edge = kblock(k * 8 + plo * 4 + pd)
        ksend[k, 0] = main
        ksend[k, 1] = edge
        main, edge = kblock(k * 8 + me)
        kgot[1 + lo, k, 0] = main
        kgot[1 + lo, k, 1] = edge

    @pl.when(jnp.logical_not(has_before))
    def _():
        kgot[0] = jnp.zeros((CHUNKS, 2, 8, LANES), jnp.float32)

        @pl.loop(0, CHUNKS * 4)
        def _(i):
            piece[i // 4, 0, i % 4] = jnp.zeros((PIECE, LANES), jnp.float32)

    @pl.when(jnp.logical_not(has_after))
    def _():
        kgot[3] = jnp.zeros((CHUNKS, 2, 8, LANES), jnp.float32)

        @pl.loop(0, CHUNKS * 4)
        def _(i):
            piece[i // 4, 3, i % 4] = jnp.zeros((PIECE, LANES), jnp.float32)

    for cp in loads:
        cp.wait()

    def build(k):
        @pl.loop(0, 8)
        def _(j):
            t = k * 8 + j
            here = pl.multiple_of(t * LANES, LANES)
            before = pl.multiple_of(jnp.maximum(t - 1, 0) * LANES, LANES)
            after = pl.multiple_of(jnp.minimum(t + 1, 15) * LANES, LANES)
            keep_left = jnp.logical_and(left, t > 0)
            keep_right = jnp.logical_and(right, t < 15)
            for f in range(2):
                packed = jnp.zeros((8, LANES), jnp.float32)
                for r in range(4):
                    for q in range(4):
                        g = q * 4 + r
                        rows = pl.ds(q * 8, 8)
                        block[t, pl.ds((f * 16 + r * 4 + q) * 8, 8), :] = slab[f, r, rows, pl.ds(here, LANES)]
                        edge = jnp.where(
                            keep_right,
                            slab[f, r, rows, pl.ds(after, LANES)],
                            jnp.where(keep_left, slab[f, r, rows, pl.ds(before, LANES)], 0.0),
                        )
                        packed = packed + (pltpu.roll(edge, 8 * g, 1) if g else edge)
                block[t, pl.ds(256 + f * 8, 8), :] = packed

    def x_copy(k, o):
        lo2, d2, dev = place(o)
        n = OFFSETS.index(o)
        return pltpu.make_async_remote_copy(
            src_ref=block.at[k * 8 + lo2 * 4 + d2],
            dst_ref=piece.at[k, 1 + lo, o[0] * 2 + o[2]],
            send_sem=xsend.at[k, n],
            recv_sem=xrecv.at[k, n],
            device_id=dev,
            device_id_type=MESH,
        )

    def x_arrival(k, o):
        lo2, d2, dev = place(o)
        n = OFFSETS.index(o)
        return pltpu.make_async_remote_copy(
            src_ref=block.at[k * 8 + lo2 * 4 + d2],
            dst_ref=piece.at[k, 1 + lo2, o[0] * 2 + o[2]],
            send_sem=xsend.at[k, n],
            recv_sem=xrecv.at[k, n],
            device_id=dev,
            device_id_type=MESH,
        )

    def own_copy(k):
        return pltpu.make_async_copy(block.at[k * 8 + me], piece.at[k, 1 + lo, 0], own_sem.at[k])

    def forward_copy(k, o, s):
        n = OFFSETS.index(o)
        q = o[0] * 2 + o[2]
        return pltpu.make_async_remote_copy(
            src_ref=piece.at[k, 1 + s, q],
            dst_ref=piece.at[k, 3 if s == 0 else 0, q],
            send_sem=zsend.at[k, n],
            recv_sem=zrecv.at[k, q, s],
            device_id=(my_lat - 2 if s == 0 else my_lat + 2, my_d),
            device_id_type=MESH,
        )

    def forward(k, o, act):
        lo2 = flip(lo, o[1])

        @pl.when(jnp.logical_and(lo2 == 0, has_before))
        def _():
            act(forward_copy(k, o, 0))

        @pl.when(jnp.logical_and(lo2 == 1, has_after))
        def _():
            act(forward_copy(k, o, 1))

    def halo_wait(k, late):
        for q in range(4):
            o = (q // 2, 0, q % 2)

            @pl.when(jnp.logical_and(has_after, lo == (0 if late else 1)))
            def _():
                forward_copy(k, o, 0).wait_recv()

            @pl.when(jnp.logical_and(has_before, lo == (1 if late else 0)))
            def _():
                forward_copy(k, o, 1).wait_recv()

    def turn_halos(k):
        halo_wait(k, False)
        turn(k, lo * 12, 4)
        halo_wait(k, True)
        turn(k, (1 - lo) * 12, 4)
        turn_edges(k)

    def k_forward(s, act):
        @pl.when(has_before if s == 0 else has_after)
        def _():
            act(
                pltpu.make_async_remote_copy(
                    src_ref=kgot.at[1 + s],
                    dst_ref=kgot.at[3 if s == 0 else 0],
                    send_sem=kz_sem.at[s],
                    recv_sem=kzrecv.at[s],
                    device_id=(my_lat - 2 if s == 0 else my_lat + 2, my_d),
                    device_id_type=MESH,
                )
            )

    def k_copy(strip):
        return pltpu.make_async_remote_copy(
            src_ref=ksend,
            dst_ref=kgot.at[1 + strip],
            send_sem=kx_sem.at[0],
            recv_sem=kx_sem.at[1],
            device_id=pdev,
            device_id_type=MESH,
        )

    near = [(0, 1, 0), (1, 1, 0), (0, 1, 1), (1, 1, 1)]
    far = [(1, 0, 0), (1, 0, 1)]
    sibling = (0, 0, 1)
    remote = [sibling] + near + far

    build(0)
    inner = jnp.logical_and(has_before, has_after)

    @pl.when(inner)
    def _():
        pl.semaphore_wait(barrier, 9)

    @pl.when(jnp.logical_not(inner))
    def _():
        pl.semaphore_wait(barrier, 8 if pairs > 1 else 7)

    start = lambda cp: cp.start()
    k_copy(lo).start()
    for o in remote:
        x_copy(0, o).start()
    own_copy(0).start()
    own_copy(0).wait()
    forward(0, (0, 0, 0), start)
    build(1)
    own_copy(1).start()
    for o in remote:
        x_copy(1, o).start()

    k_copy(1 - lo).wait_recv()
    k_forward(0, start)
    k_forward(1, start)

    def arrive(k, o):
        x_arrival(k, o).wait_recv()
        forward(k, o, start)

    arrive(0, sibling)
    own_copy(1).wait()

    def k_received():
        @pl.when(has_after)
        def _():
            pltpu.make_async_remote_copy(
                src_ref=kgot.at[1], dst_ref=kgot.at[3], send_sem=kz_sem.at[0], recv_sem=kzrecv.at[0],
                device_id=(my_lat - 2, my_d), device_id_type=MESH,
            ).wait_recv()

        @pl.when(has_before)
        def _():
            pltpu.make_async_remote_copy(
                src_ref=kgot.at[2], dst_ref=kgot.at[0], send_sem=kz_sem.at[1], recv_sem=kzrecv.at[1],
                device_id=(my_lat + 2, my_d), device_id_type=MESH,
            ).wait_recv()

    sub = lax.broadcasted_iota(jnp.int32, (8, LANES), 0)

    def put_edges(edges, dst, row):
        dst[row, FIRST - 8:FIRST] = jnp.where(sub >= 4, edges[(row + 15) % 16 * 8:(row + 15) % 16 * 8 + 8], 0.0)
        dst[row, LAST:LAST + 8] = jnp.where(sub < 4, edges[row * 8:row * 8 + 8], 0.0)

    def diffusivities(k):
        for kind in range(2):
            dst = coef.at[k, kind]

            @pl.loop(0, 16)
            def _(r):
                line = kgot[r // 4, k, 0, pl.ds(kind * 4 + r % 4, 1), :]
                dst[r, FIRST:LAST] = 0.25 * jnp.broadcast_to(line, (LANES, LANES)).T

            edges = jnp.zeros((8, LANES), jnp.float32)
            for r in range(16):
                line = jnp.broadcast_to(kgot[r // 4, k, 1, kind * 4 + r % 4:kind * 4 + r % 4 + 1, :], (8, LANES))
                edges = edges + (pltpu.roll(line, 8 * r, 1) if r else line)
            edges = 0.25 * jnp.broadcast_to(edges[0:1], (LANES, LANES)).T
            for r in range(16):
                put_edges(edges, dst, r)

    def slot(d):
        h2, c2 = d // 2, d % 2
        return ((1 - hi) if h2 else hi) * 2 + ((1 - core) if c2 else core)

    def turn(k, first, count):
        slots = [slot(d) for d in range(4)]

        @pl.loop(0, 2 * count)
        def _(i):
            f, row = i // count, first + i % count
            rows = pl.ds(pl.multiple_of(f * 128 + row % 4 * 32, 32), 32)
            levels = jnp.concatenate([piece[k, row // 4, q, rows, :] for q in slots], axis=0)
            turned[0, f, row, FIRST:LAST] = levels.T

    def turn_edges(k):
        slots = [slot(d) for d in range(4)]
        for f in range(2):
            blocks = []
            for q in slots:
                packs = [piece[k, strip, q, 256 + f * 8:264 + f * 8, :] for strip in range(4)]
                for tile in range(4):
                    total = jnp.zeros((8, LANES), jnp.float32)
                    for strip in range(4):
                        shift = 32 * (strip - tile) % LANES
                        moved = pltpu.roll(packs[strip], shift, 1) if shift else packs[strip]
                        inside = (lane + 4) % LANES // 32 == strip
                        total = jnp.where(inside, moved, total)
                    blocks.append(total)
            edges = jnp.concatenate(blocks, axis=0).T
            for r in range(16):
                put_edges(edges, turned.at[0, f], r)

    def stencil(k):
        for t in range(LSUB):
            src, dst = turned.at[t % 2], turned.at[1 - t % 2]
            last = t == LSUB - 1

            @pl.loop(t + 1, 15 - t)
            def _(r):
                for s in range(FIRST if last else FIRST - 8, LAST if last else LAST + 8, 8):
                    def lap(f, centre):
                        return (
                            src[f, r + 1, s:s + 8] + src[f, r - 1, s:s + 8]
                            + src[f, r, s + 1:s + 9] + src[f, r, s - 1:s + 7] - 4.0 * centre
                        )

                    h, w = src[0, r, s:s + 8], src[1, r, s:s + 8]
                    factor = coef[k, 0, r, s:s + 8] * (1.5 - 0.5 / (1.0 + w * w))
                    h2 = h + factor * lap(0, h)
                    w2 = w + coef[k, 1, r, s:s + 8] * lap(1, w)
                    if last:
                        state[k, 0, r - 4, s - FIRST:s - FIRST + 8] = h2
                        state[k, 1, r - 4, s - FIRST:s - FIRST + 8] = w2
                    else:
                        dst[0, r, s:s + 8] = h2
                        dst[1, r, s:s + 8] = w2

    def r_copy(k, half, o):
        lo2, d2, dev = place(o)
        n = OFFSETS.index(o)
        return pltpu.make_async_remote_copy(
            src_ref=solved.at[k, :, pl.ds(lo2 * 4 + half * 2, 2), pl.ds(pl.multiple_of(d2 * SLAB, SLAB), SLAB), :],
            dst_ref=result.at[:, pl.ds(half * 2, 2), :, pl.ds(pl.multiple_of((k * 8 + me) * LANES, LANES), LANES)],
            send_sem=rsend.at[k, half, n],
            recv_sem=rrecv.at[k, half, n],
            device_id=dev,
            device_id_type=MESH,
        )

    def r_arrival(k, half, o):
        lo2, d2, dev = place(o)
        n = OFFSETS.index(o)
        src = (k * 8 + lo2 * 4 + d2) * LANES
        return pltpu.make_async_remote_copy(
            src_ref=solved.at[k, :, pl.ds(lo2 * 4 + half * 2, 2), pl.ds(pl.multiple_of(d2 * SLAB, SLAB), SLAB), :],
            dst_ref=result.at[:, pl.ds(half * 2, 2), :, pl.ds(pl.multiple_of(src, LANES), LANES)],
            send_sem=rsend.at[k, half, n],
            recv_sem=rrecv.at[k, half, n],
            device_id=dev,
            device_id_type=MESH,
        )

    def r_own(k, half):
        return pltpu.make_async_copy(
            solved.at[k, :, pl.ds(lo * 4 + half * 2, 2), pl.ds(pl.multiple_of(my_d * SLAB, SLAB), SLAB), :],
            result.at[:, pl.ds(half * 2, 2), :, pl.ds(pl.multiple_of((k * 8 + me) * LANES, LANES), LANES)],
            rown_sem.at[k, half],
        )

    def solve(k):
        for half in range(2):
            for l in (1, 0):
                rp = flip(lo, l) * 2 + half
                fields = [[], []]
                for r in range(2):
                    h, w = state[k, 0, rp * 2 + r], state[k, 1, rp * 2 + r]
                    kw = w * coef[k, 1, rp * 2 + r + 4, FIRST:LAST]
                    fields[0].append(jnp.concatenate([h, kw], axis=1))
                    fields[1].append(jnp.concatenate([w, kw], axis=1))
                temp, moist = (
                    lax.dot_general(
                        mats[n], jnp.concatenate(fields[n], axis=0), (((1,), (1,)), ((), ())),
                        precision=highest, preferred_element_type=jnp.float32,
                    )
                    for n in range(2)
                )
                for f, out in enumerate((temp, moist)):
                    solved[k, f, rp * 2] = out[:, :LANES]
                    solved[k, f, rp * 2 + 1] = out[:, LANES:]
                for o in [(1, l, 0), (1, l, 1), (0, l, 0), (0, l, 1)]:
                    if o == (0, 0, 0):
                        r_own(k, half).start()
                    else:
                        r_copy(k, half, o).start()

    k_received()
    arrive(0, near[0])
    arrive(0, near[1])
    diffusivities(0)
    arrive(0, near[2])
    arrive(0, near[3])
    diffusivities(1)
    highest = lax.Precision.HIGHEST
    mats[0, :, 0:LEVELS] = thermal_ref[...]
    mats[1, :, 0:LEVELS] = water_ref[...]
    mats[0, :, LEVELS:] = -1.0 * jnp.dot(thermal_ref[...], deriv_ref[...], precision=highest, preferred_element_type=jnp.float32)
    mats[1, :, LEVELS:] = 2.0 * jnp.dot(water_ref[...], deriv_ref[...], precision=highest, preferred_element_type=jnp.float32)

    for o in far:
        arrive(0, o)
    forward(1, (0, 0, 0), start)
    arrive(1, sibling)
    turn(0, 4, 8)
    arrive(1, near[0])
    arrive(1, near[1])
    turn_halos(0)
    arrive(1, near[2])
    arrive(1, near[3])
    stencil(0)
    arrive(1, far[0])
    solve(0)
    arrive(1, far[1])
    turn(1, 4, 8)
    turn_halos(1)
    stencil(1)
    solve(1)

    def store(k, half):
        cols = pl.ds(k * 8 * LANES, 8 * LANES)
        copies = []
        for f, out in enumerate((heat_out, wet_out)):
            for r in (half * 2, half * 2 + 1):
                copies.append(pltpu.make_async_copy(result.at[f, r, :, cols], out.at[:, r, cols], store_sem.at[k, f * 4 + r]))
        return copies

    for k in range(CHUNKS):
        for half in range(2):
            r_own(k, half).wait()
            for o in remote:
                r_arrival(k, half, o).wait_recv()
            for cp in store(k, half):
                cp.start()

    k_copy(lo).wait_send()
    k_forward(0, lambda cp: cp.wait_send())
    k_forward(1, lambda cp: cp.wait_send())
    for k in range(CHUNKS):
        for o in remote:
            x_copy(k, o).wait_send()
        for o in OFFSETS:
            forward(k, o, lambda cp: cp.wait_send())
        for half in range(2):
            for o in remote:
                r_copy(k, half, o).wait_send()
            for cp in store(k, half):
                cp.wait()


def solution(mesh):
    pairs = mesh.shape["lat"] // 2
    deriv = scaled_derivative()

    def per_device(heat, wet, label, spread, factor, thermal, water):
        any_spec = pl.BlockSpec(memory_space=pl.ANY)
        vmem = pl.BlockSpec(memory_space=pltpu.VMEM)
        smem = pl.BlockSpec(memory_space=pltpu.SMEM)
        dma = pltpu.SemaphoreType.DMA
        f32 = jnp.float32
        out = jax.ShapeDtypeStruct(heat.shape, f32)
        return pl.pallas_call(
            functools.partial(kernel, pairs),
            out_shape=(out, out),
            in_specs=[any_spec, any_spec, vmem, smem, smem, vmem, vmem, vmem],
            out_specs=(any_spec, any_spec),
            scratch_shapes=[
                pltpu.VMEM((2, 4, SLAB, 16 * LANES), f32),
                pltpu.VMEM((16, PIECE, LANES), f32),
                pltpu.VMEM((CHUNKS, 4, 4, PIECE, LANES), f32),
                pltpu.VMEM((18, 8, LANES), f32),
                pltpu.VMEM((CHUNKS, 2, 8, LANES), f32),
                pltpu.VMEM((4, CHUNKS, 2, 8, LANES), f32),
                pltpu.VMEM((CHUNKS, 2, 16, SPAN, LANES), f32),
                pltpu.VMEM((2, 2, 16, SPAN, LANES), f32),
                pltpu.VMEM((CHUNKS, 2, 8, LANES, LEVELS), f32),
                pltpu.VMEM((CHUNKS, 2, 8, LEVELS, LANES), f32),
                pltpu.VMEM((2, 4, SLAB, 16 * LANES), f32),
                pltpu.VMEM((2, LEVELS, 2 * LEVELS), f32),
                dma((8,)),
                dma((CHUNKS,)),
                dma((CHUNKS, 8)),
                dma((CHUNKS, 8)),
                dma((CHUNKS, 8)),
                dma((CHUNKS, 4, 2)),
                dma((1,)),
                dma((2,)),
                dma((2,)),
                dma((2,)),
                dma((CHUNKS, 2)),
                dma((CHUNKS, 2, 8)),
                dma((CHUNKS, 2, 8)),
                dma((CHUNKS, 8)),
            ],
            compiler_params=pltpu.CompilerParams(
                collective_id=0, has_side_effects=True, vmem_limit_bytes=48 << 20
            ),
        )(*(pltpu.with_memory_space_constraint(x, pltpu.HBM) for x in (heat, wet, label, spread, factor, thermal, water, jnp.asarray(deriv))))

    return jax.shard_map(
        per_device,
        mesh=mesh,
        in_specs=(
            P("depth", "lat", None),
            P("depth", "lat", None),
            P("lat", None),
            P(),
            P(),
            P(),
            P(),
        ),
        out_specs=(P("depth", "lat", None), P("depth", "lat", None)),
        check_vma=False,
    )
```

```python
import functools

import jax
import jax.numpy as jnp
import numpy as np
from jax import lax
from jax.experimental import pallas as pl
from jax.experimental.pallas import tpu as pltpu
from jax.sharding import PartitionSpec as P

MESH = pl.DeviceIdType.MESH
LEVELS = 128
CLASSES = 12
LSUB = 4
CHUNKS = 2
LANES = 128
SLAB = 32
PIECE = 272
FIRST, LAST = 16, 16 + LANES
SPAN = LAST + 16
OFFSETS = [(h, l, c) for h in (0, 1) for l in (0, 1) for c in (0, 1)]


def scaled_derivative():
    f32 = np.float32
    index = np.arange(LEVELS).astype(f32)
    nodes = np.cos(f32(np.pi) * index / f32(LEVELS - 1)).astype(f32)
    ends = np.where((index == 0) | (index == LEVELS - 1), 2.0, 1.0)
    signs = np.where(np.arange(LEVELS) % 2 == 0, 1.0, -1.0)
    weight = (ends * signs).astype(f32)
    diagonal = np.eye(LEVELS, dtype=bool)
    spread = nodes[:, None] - nodes[None, :]
    off = weight[:, None] / weight[None, :] / np.where(diagonal, f32(1), spread)
    off = np.where(diagonal, f32(0), off)
    deriv = off - np.diag(np.sum(off, axis=1))
    scale = (f32(1) - nodes * nodes) / f32(LEVELS)
    return (scale[:, None] * deriv).astype(f32)


def flip(value, bit):
    return 1 - value if bit else value


def kernel(
    pairs,
    heat_ref, wet_ref, label_ref, spread_ref, factor_ref, thermal_ref, water_ref, deriv_ref,
    heat_out, wet_out,
    slab, block, piece, kloc, ksend, kgot, coef, turned, state, solved, result, mats,
    load_sem, own_sem, xsend, xrecv, zsend, zrecv, kown_sem, kx_sem, kz_sem, kzrecv, rown_sem, rsend, rrecv, store_sem,
):
    my_lat = lax.axis_index("lat")
    my_d = lax.axis_index("depth")
    pair, lo = my_lat // 2, my_lat % 2
    hi, core = my_d // 2, my_d % 2
    me = lo * 4 + my_d
    has_before, has_after = pair > 0, pair < pairs - 1

    def place(o):
        h, l, c = o
        lo2 = flip(lo, l)
        d2 = flip(hi, h) * 2 + flip(core, c)
        return lo2, d2, (pair * 2 + lo2, d2)

    loads = []
    for f, src in enumerate((heat_ref, wet_ref)):
        for r in range(4):
            loads.append(pltpu.make_async_copy(src.at[:, r, :], slab.at[f, r], load_sem.at[f * 4 + r]))
    for cp in loads:
        cp.start()

    barrier = pltpu.get_barrier_semaphore()
    for o in OFFSETS[1:]:
        pl.semaphore_signal(barrier, inc=1, device_id=place(o)[2], device_id_type=MESH)

    @pl.when(has_before)
    def _():
        pl.semaphore_signal(barrier, inc=1, device_id=(my_lat - 2, my_d), device_id_type=MESH)

    @pl.when(has_after)
    def _():
        pl.semaphore_signal(barrier, inc=1, device_id=(my_lat + 2, my_d), device_id_type=MESH)

    lane = lax.broadcasted_iota(jnp.int32, (8, LANES), 1)
    right, left = lane < 4, lane >= LANES - 4

    kloc[0] = jnp.zeros((8, LANES), jnp.float32)
    kloc[17] = jnp.zeros((8, LANES), jnp.float32)
    for t in range(16):
        label = label_ref[:, t * LANES:(t + 1) * LANES]
        kh = jnp.zeros((4, LANES), jnp.float32)
        km = jnp.zeros((4, LANES), jnp.float32)
        for n in range(CLASSES):
            kh = jnp.where(label == n, spread_ref[n], kh)
            km = jnp.where(label == n, factor_ref[n], km)
        kloc[t + 1, 0:4] = kh
        kloc[t + 1, 4:8] = km

    def kblock(t):
        main = kloc[t + 1]
        edge = jnp.where(right, kloc[t + 2], jnp.where(left, kloc[t], 0.0))
        return main, edge

    partner = (0, 1, 0)
    plo, pd, pdev = place(partner)
    for k in range(CHUNKS):
        main, edge = kblock(k * 8 + plo * 4 + pd)
        ksend[k, 0] = main
        ksend[k, 1] = edge
        main, edge = kblock(k * 8 + me)
        kgot[1 + lo, k, 0] = main
        kgot[1 + lo, k, 1] = edge

    @pl.when(jnp.logical_not(has_before))
    def _():
        kgot[0] = jnp.zeros((CHUNKS, 2, 8, LANES), jnp.float32)

        @pl.loop(0, CHUNKS * 4)
        def _(i):
            piece[i // 4, 0, i % 4] = jnp.zeros((PIECE, LANES), jnp.float32)

    @pl.when(jnp.logical_not(has_after))
    def _():
        kgot[3] = jnp.zeros((CHUNKS, 2, 8, LANES), jnp.float32)

        @pl.loop(0, CHUNKS * 4)
        def _(i):
            piece[i // 4, 3, i % 4] = jnp.zeros((PIECE, LANES), jnp.float32)

    for cp in loads:
        cp.wait()

    def build(k):
        @pl.loop(0, 8)
        def _(j):
            t = k * 8 + j
            here = pl.multiple_of(t * LANES, LANES)
            before = pl.multiple_of(jnp.maximum(t - 1, 0) * LANES, LANES)
            after = pl.multiple_of(jnp.minimum(t + 1, 15) * LANES, LANES)
            keep_left = jnp.logical_and(left, t > 0)
            keep_right = jnp.logical_and(right, t < 15)
            for f in range(2):
                packed = jnp.zeros((8, LANES), jnp.float32)
                for r in range(4):
                    for q in range(4):
                        g = q * 4 + r
                        rows = pl.ds(q * 8, 8)
                        block[t, pl.ds((f * 16 + r * 4 + q) * 8, 8), :] = slab[f, r, rows, pl.ds(here, LANES)]
                        edge = jnp.where(
                            keep_right,
                            slab[f, r, rows, pl.ds(after, LANES)],
                            jnp.where(keep_left, slab[f, r, rows, pl.ds(before, LANES)], 0.0),
                        )
                        packed = packed + (pltpu.roll(edge, 8 * g, 1) if g else edge)
                block[t, pl.ds(256 + f * 8, 8), :] = packed

    def x_copy(k, o):
        lo2, d2, dev = place(o)
        n = OFFSETS.index(o)
        return pltpu.make_async_remote_copy(
            src_ref=block.at[k * 8 + lo2 * 4 + d2],
            dst_ref=piece.at[k, 1 + lo, o[0] * 2 + o[2]],
            send_sem=xsend.at[k, n],
            recv_sem=xrecv.at[k, n],
            device_id=dev,
            device_id_type=MESH,
        )

    def x_arrival(k, o):
        lo2, d2, dev = place(o)
        n = OFFSETS.index(o)
        return pltpu.make_async_remote_copy(
            src_ref=block.at[k * 8 + lo2 * 4 + d2],
            dst_ref=piece.at[k, 1 + lo2, o[0] * 2 + o[2]],
            send_sem=xsend.at[k, n],
            recv_sem=xrecv.at[k, n],
            device_id=dev,
            device_id_type=MESH,
        )

    def own_copy(k):
        return pltpu.make_async_copy(block.at[k * 8 + me], piece.at[k, 1 + lo, 0], own_sem.at[k])

    def forward_copy(k, o, s):
        n = OFFSETS.index(o)
        q = o[0] * 2 + o[2]
        return pltpu.make_async_remote_copy(
            src_ref=piece.at[k, 1 + s, q],
            dst_ref=piece.at[k, 3 if s == 0 else 0, q],
            send_sem=zsend.at[k, n],
            recv_sem=zrecv.at[k, q, s],
            device_id=(my_lat - 2 if s == 0 else my_lat + 2, my_d),
            device_id_type=MESH,
        )

    def forward(k, o, act):
        lo2 = flip(lo, o[1])

        @pl.when(jnp.logical_and(lo2 == 0, has_before))
        def _():
            act(forward_copy(k, o, 0))

        @pl.when(jnp.logical_and(lo2 == 1, has_after))
        def _():
            act(forward_copy(k, o, 1))

    def halo_wait(k, late):
        for q in range(4):
            o = (q // 2, 0, q % 2)

            @pl.when(jnp.logical_and(has_after, lo == (0 if late else 1)))
            def _():
                forward_copy(k, o, 0).wait_recv()

            @pl.when(jnp.logical_and(has_before, lo == (1 if late else 0)))
            def _():
                forward_copy(k, o, 1).wait_recv()

    def turn_halos(k):
        halo_wait(k, False)
        turn(k, lo * 12, 4)
        halo_wait(k, True)
        turn(k, (1 - lo) * 12, 4)
        turn_edges(k)

    def k_forward(s, act):
        @pl.when(has_before if s == 0 else has_after)
        def _():
            act(
                pltpu.make_async_remote_copy(
                    src_ref=kgot.at[1 + s],
                    dst_ref=kgot.at[3 if s == 0 else 0],
                    send_sem=kz_sem.at[s],
                    recv_sem=kzrecv.at[s],
                    device_id=(my_lat - 2 if s == 0 else my_lat + 2, my_d),
                    device_id_type=MESH,
                )
            )

    def k_copy(strip):
        return pltpu.make_async_remote_copy(
            src_ref=ksend,
            dst_ref=kgot.at[1 + strip],
            send_sem=kx_sem.at[0],
            recv_sem=kx_sem.at[1],
            device_id=pdev,
            device_id_type=MESH,
        )

    near = [(0, 1, 0), (1, 1, 0), (0, 1, 1), (1, 1, 1)]
    far = [(1, 0, 0), (1, 0, 1)]
    sibling = (0, 0, 1)
    remote = [sibling] + near + far

    build(0)
    inner = jnp.logical_and(has_before, has_after)

    @pl.when(inner)
    def _():
        pl.semaphore_wait(barrier, 9)

    @pl.when(jnp.logical_not(inner))
    def _():
        pl.semaphore_wait(barrier, 8 if pairs > 1 else 7)

    start = lambda cp: cp.start()
    k_copy(lo).start()
    for o in remote:
        x_copy(0, o).start()
    own_copy(0).start()
    own_copy(0).wait()
    forward(0, (0, 0, 0), start)
    build(1)
    own_copy(1).start()
    for o in remote:
        x_copy(1, o).start()

    k_copy(1 - lo).wait_recv()
    k_forward(0, start)
    k_forward(1, start)

    def arrive(k, o):
        x_arrival(k, o).wait_recv()
        forward(k, o, start)

    arrive(0, sibling)
    own_copy(1).wait()

    def k_received():
        @pl.when(has_after)
        def _():
            pltpu.make_async_remote_copy(
                src_ref=kgot.at[1], dst_ref=kgot.at[3], send_sem=kz_sem.at[0], recv_sem=kzrecv.at[0],
                device_id=(my_lat - 2, my_d), device_id_type=MESH,
            ).wait_recv()

        @pl.when(has_before)
        def _():
            pltpu.make_async_remote_copy(
                src_ref=kgot.at[2], dst_ref=kgot.at[0], send_sem=kz_sem.at[1], recv_sem=kzrecv.at[1],
                device_id=(my_lat + 2, my_d), device_id_type=MESH,
            ).wait_recv()

    sub = lax.broadcasted_iota(jnp.int32, (8, LANES), 0)

    def put_edges(edges, dst, row):
        dst[row, FIRST - 8:FIRST] = jnp.where(sub >= 4, edges[(row + 15) % 16 * 8:(row + 15) % 16 * 8 + 8], 0.0)
        dst[row, LAST:LAST + 8] = jnp.where(sub < 4, edges[row * 8:row * 8 + 8], 0.0)

    def diffusivities(k):
        for kind in range(2):
            dst = coef.at[k, kind]

            @pl.loop(0, 16)
            def _(r):
                line = kgot[r // 4, k, 0, pl.ds(kind * 4 + r % 4, 1), :]
                dst[r, FIRST:LAST] = 0.25 * jnp.broadcast_to(line, (LANES, LANES)).T

            edges = jnp.zeros((8, LANES), jnp.float32)
            for r in range(16):
                line = jnp.broadcast_to(kgot[r // 4, k, 1, kind * 4 + r % 4:kind * 4 + r % 4 + 1, :], (8, LANES))
                edges = edges + (pltpu.roll(line, 8 * r, 1) if r else line)
            edges = 0.25 * jnp.broadcast_to(edges[0:1], (LANES, LANES)).T
            for r in range(16):
                put_edges(edges, dst, r)

    def slot(d):
        h2, c2 = d // 2, d % 2
        return ((1 - hi) if h2 else hi) * 2 + ((1 - core) if c2 else core)

    def turn(k, first, count):
        slots = [slot(d) for d in range(4)]

        @pl.loop(0, 2 * count)
        def _(i):
            f, row = i // count, first + i % count
            rows = pl.ds(pl.multiple_of(f * 128 + row % 4 * 32, 32), 32)
            levels = jnp.concatenate([piece[k, row // 4, q, rows, :] for q in slots], axis=0)
            turned[0, f, row, FIRST:LAST] = levels.T

    def turn_edges(k):
        slots = [slot(d) for d in range(4)]
        for f in range(2):
            blocks = []
            for q in slots:
                packs = [piece[k, strip, q, 256 + f * 8:264 + f * 8, :] for strip in range(4)]
                for tile in range(4):
                    total = jnp.zeros((8, LANES), jnp.float32)
                    for strip in range(4):
                        shift = 32 * (strip - tile) % LANES
                        moved = pltpu.roll(packs[strip], shift, 1) if shift else packs[strip]
                        inside = (lane + 4) % LANES // 32 == strip
                        total = jnp.where(inside, moved, total)
                    blocks.append(total)
            edges = jnp.concatenate(blocks, axis=0).T
            for r in range(16):
                put_edges(edges, turned.at[0, f], r)

    def stencil(k):
        for t in range(LSUB):
            src, dst = turned.at[t % 2], turned.at[1 - t % 2]
            last = t == LSUB - 1

            @pl.loop(t + 1, 15 - t)
            def _(r):
                for s in range(FIRST if last else FIRST - 8, LAST if last else LAST + 8, 8):
                    def lap(f, centre):
                        return (
                            src[f, r + 1, s:s + 8] + src[f, r - 1, s:s + 8]
                            + src[f, r, s + 1:s + 9] + src[f, r, s - 1:s + 7] - 4.0 * centre
                        )

                    h, w = src[0, r, s:s + 8], src[1, r, s:s + 8]
                    factor = coef[k, 0, r, s:s + 8] * (1.5 - 0.5 / (1.0 + w * w))
                    h2 = h + factor * lap(0, h)
                    w2 = w + coef[k, 1, r, s:s + 8] * lap(1, w)
                    if last:
                        state[k, 0, r - 4, s - FIRST:s - FIRST + 8] = h2
                        state[k, 1, r - 4, s - FIRST:s - FIRST + 8] = w2
                    else:
                        dst[0, r, s:s + 8] = h2
                        dst[1, r, s:s + 8] = w2

    def r_copy(k, half, o):
        lo2, d2, dev = place(o)
        n = OFFSETS.index(o)
        return pltpu.make_async_remote_copy(
            src_ref=solved.at[k, :, pl.ds(lo2 * 4 + half * 2, 2), pl.ds(pl.multiple_of(d2 * SLAB, SLAB), SLAB), :],
            dst_ref=result.at[:, pl.ds(half * 2, 2), :, pl.ds(pl.multiple_of((k * 8 + me) * LANES, LANES), LANES)],
            send_sem=rsend.at[k, half, n],
            recv_sem=rrecv.at[k, half, n],
            device_id=dev,
            device_id_type=MESH,
        )

    def r_arrival(k, half, o):
        lo2, d2, dev = place(o)
        n = OFFSETS.index(o)
        src = (k * 8 + lo2 * 4 + d2) * LANES
        return pltpu.make_async_remote_copy(
            src_ref=solved.at[k, :, pl.ds(lo2 * 4 + half * 2, 2), pl.ds(pl.multiple_of(d2 * SLAB, SLAB), SLAB), :],
            dst_ref=result.at[:, pl.ds(half * 2, 2), :, pl.ds(pl.multiple_of(src, LANES), LANES)],
            send_sem=rsend.at[k, half, n],
            recv_sem=rrecv.at[k, half, n],
            device_id=dev,
            device_id_type=MESH,
        )

    def r_own(k, half):
        return pltpu.make_async_copy(
            solved.at[k, :, pl.ds(lo * 4 + half * 2, 2), pl.ds(pl.multiple_of(my_d * SLAB, SLAB), SLAB), :],
            result.at[:, pl.ds(half * 2, 2), :, pl.ds(pl.multiple_of((k * 8 + me) * LANES, LANES), LANES)],
            rown_sem.at[k, half],
        )

    def solve(k):
        for half in range(2):
            for l in (0, 1):
                rp = flip(lo, l) * 2 + half
                fields = [[], []]
                for r in range(2):
                    h, w = state[k, 0, rp * 2 + r], state[k, 1, rp * 2 + r]
                    kw = w * coef[k, 1, rp * 2 + r + 4, FIRST:LAST]
                    fields[0].append(jnp.concatenate([h, kw], axis=1))
                    fields[1].append(jnp.concatenate([w, kw], axis=1))
                temp, moist = (
                    lax.dot_general(
                        mats[n], jnp.concatenate(fields[n], axis=0), (((1,), (1,)), ((), ())),
                        precision=highest, preferred_element_type=jnp.float32,
                    )
                    for n in range(2)
                )
                for f, out in enumerate((temp, moist)):
                    solved[k, f, rp * 2] = out[:, :LANES]
                    solved[k, f, rp * 2 + 1] = out[:, LANES:]
                for o in [(1, l, 0), (1, l, 1), (0, l, 0), (0, l, 1)]:
                    if o == (0, 0, 0):
                        r_own(k, half).start()
                    else:
                        r_copy(k, half, o).start()

    k_received()
    arrive(0, near[0])
    arrive(0, near[1])
    diffusivities(0)
    arrive(0, near[2])
    arrive(0, near[3])
    diffusivities(1)
    highest = lax.Precision.HIGHEST
    mats[0, :, 0:LEVELS] = thermal_ref[...]
    mats[1, :, 0:LEVELS] = water_ref[...]
    mats[0, :, LEVELS:] = -1.0 * jnp.dot(thermal_ref[...], deriv_ref[...], precision=highest, preferred_element_type=jnp.float32)
    mats[1, :, LEVELS:] = 2.0 * jnp.dot(water_ref[...], deriv_ref[...], precision=highest, preferred_element_type=jnp.float32)

    for o in far:
        arrive(0, o)
    forward(1, (0, 0, 0), start)
    arrive(1, sibling)
    turn(0, 4, 8)
    arrive(1, near[0])
    arrive(1, near[1])
    turn_halos(0)
    arrive(1, near[2])
    arrive(1, near[3])
    stencil(0)
    arrive(1, far[0])
    solve(0)
    arrive(1, far[1])
    turn(1, 4, 8)
    turn_halos(1)
    stencil(1)
    solve(1)

    def store(k, half):
        cols = pl.ds(k * 8 * LANES, 8 * LANES)
        copies = []
        for f, out in enumerate((heat_out, wet_out)):
            for r in (half * 2, half * 2 + 1):
                copies.append(pltpu.make_async_copy(result.at[f, r, :, cols], out.at[:, r, cols], store_sem.at[k, f * 4 + r]))
        return copies

    for k in range(CHUNKS):
        for half in range(2):
            r_own(k, half).wait()
            for o in remote:
                r_arrival(k, half, o).wait_recv()
            for cp in store(k, half):
                cp.start()

    k_copy(lo).wait_send()
    k_forward(0, lambda cp: cp.wait_send())
    k_forward(1, lambda cp: cp.wait_send())
    for k in range(CHUNKS):
        for o in remote:
            x_copy(k, o).wait_send()
        for o in OFFSETS:
            forward(k, o, lambda cp: cp.wait_send())
        for half in range(2):
            for o in remote:
                r_copy(k, half, o).wait_send()
            for cp in store(k, half):
                cp.wait()


def solution(mesh):
    pairs = mesh.shape["lat"] // 2
    deriv = scaled_derivative()

    def per_device(heat, wet, label, spread, factor, thermal, water):
        any_spec = pl.BlockSpec(memory_space=pl.ANY)
        vmem = pl.BlockSpec(memory_space=pltpu.VMEM)
        smem = pl.BlockSpec(memory_space=pltpu.SMEM)
        dma = pltpu.SemaphoreType.DMA
        f32 = jnp.float32
        out = jax.ShapeDtypeStruct(heat.shape, f32)
        return pl.pallas_call(
            functools.partial(kernel, pairs),
            out_shape=(out, out),
            in_specs=[any_spec, any_spec, vmem, smem, smem, vmem, vmem, vmem],
            out_specs=(any_spec, any_spec),
            scratch_shapes=[
                pltpu.VMEM((2, 4, SLAB, 16 * LANES), f32),
                pltpu.VMEM((16, PIECE, LANES), f32),
                pltpu.VMEM((CHUNKS, 4, 4, PIECE, LANES), f32),
                pltpu.VMEM((18, 8, LANES), f32),
                pltpu.VMEM((CHUNKS, 2, 8, LANES), f32),
                pltpu.VMEM((4, CHUNKS, 2, 8, LANES), f32),
                pltpu.VMEM((CHUNKS, 2, 16, SPAN, LANES), f32),
                pltpu.VMEM((2, 2, 16, SPAN, LANES), f32),
                pltpu.VMEM((CHUNKS, 2, 8, LANES, LEVELS), f32),
                pltpu.VMEM((CHUNKS, 2, 8, LEVELS, LANES), f32),
                pltpu.VMEM((2, 4, SLAB, 16 * LANES), f32),
                pltpu.VMEM((2, LEVELS, 2 * LEVELS), f32),
                dma((8,)),
                dma((CHUNKS,)),
                dma((CHUNKS, 8)),
                dma((CHUNKS, 8)),
                dma((CHUNKS, 8)),
                dma((CHUNKS, 4, 2)),
                dma((1,)),
                dma((2,)),
                dma((2,)),
                dma((2,)),
                dma((CHUNKS, 2)),
                dma((CHUNKS, 2, 8)),
                dma((CHUNKS, 2, 8)),
                dma((CHUNKS, 8)),
            ],
            compiler_params=pltpu.CompilerParams(
                collective_id=0, has_side_effects=True, vmem_limit_bytes=48 << 20
            ),
        )(*(pltpu.with_memory_space_constraint(x, pltpu.HBM) for x in (heat, wet, label, spread, factor, thermal, water, jnp.asarray(deriv))))

    return jax.shard_map(
        per_device,
        mesh=mesh,
        in_specs=(
            P("depth", "lat", None),
            P("depth", "lat", None),
            P("lat", None),
            P(),
            P(),
            P(),
            P(),
        ),
        out_specs=(P("depth", "lat", None), P("depth", "lat", None)),
        check_vma=False,
    )
```
